512 devices in a mesh: row: 8 (over x, z_hi), col: 64 (over y, z_lo, core).
Axes of the slice: x: 4, y: 8, z: 8 (z_hi: 2, z_lo: 4; z = z_hi * 4 + z_lo), core: 2. Of those that a mesh axis runs over, the one named last changes fastest.
Arguments:
- features: float32 [64, 1024, 128], P('col'), may hold values from -6 to 6
- self_weight: float32 [128, 256], replicated, may hold values from -0.5 to 0.5
- neigh_weight: float32 [128, 256], replicated, may hold values from -0.5 to 0.5
- bias: float32 [256], replicated, may hold values from -4 to 4
- edge_tiles: bfloat16 [8, 64, 96, 128, 128], P('row', 'col'), may hold values from -0.078125 to 0.078125
- tile_rows: int32 [8, 64, 96], P('row', 'col'), may hold values from 0 to 7
- tile_cols: int32 [8, 64, 96], P('row', 'col'), may hold values from 0 to 7
- tile_count: int32 [8, 64, 8], P('row', 'col'), may hold values from 1 to 12, as said below
- cotangent: float32 [64, 1024, 256], P('col', 'row'), may hold values from -6 to 6
Outputs:
- output: float32 [64, 1024, 256], P('col', 'row')
- grad_self: float32 [128, 256], replicated
- grad_neigh: float32 [128, 256], replicated
- grad_bias: float32 [256], replicated
The draws below stay inside these ranges and needn't reach their ends.
Inputs may be any that keep to these rules, and one draw needn't show every extreme that they name: tile_count reaches 12 in every draw.
All inputs are finite; a program needn't handle non-finite values.
Results may differ from the reference program's by a relative error of at most 0.0003.
Values sent between devices are 32-bit elements; how exact they have to be, the bound alone decides.
A program may use at most 64 MiB of HBM per device.

```python
import jax
import jax.numpy as jnp
from jax import lax

DIN = 128
DOUT = 256
TILE = 128
KT = 8
TS = 12
STOPS = 8
G = 1024
NODES = 65536
N_ROW = 8
N_COL = 64


def draw_tile_count(key, part):
    counts = jax.random.randint(key, (N_ROW, N_COL, STOPS), 1, TS + 1)
    return counts.at[0, 0, 0].set(TS).astype(jnp.int32)


def plant(drawn, own_key, low, high):
    longest = drawn.shape.index(max(drawn.shape))
    spots = []
    for shift in (0, 1):
        where = [jax.random.randint(jax.random.fold_in(own_key, axis), (), 0, length) for axis, length in enumerate(drawn.shape)]
        where[longest] = (where[longest] + shift) % drawn.shape[longest]
        spots.append(tuple(where))
    return drawn.at[spots[0]].set(low).at[spots[1]].set(high)


def steps_of(key, dims, pieces, low, top_value):
    factor_of = 1.0
    for axis_at, blocks in pieces:
        draws = jax.random.uniform(jax.random.fold_in(jax.random.fold_in(key, 6), axis_at), (blocks,), jnp.float32, low / len(pieces), top_value / len(pieces))
        factor_of = factor_of * jnp.repeat(jnp.exp(draws), dims[axis_at] // blocks).reshape((-1,) + (1,) * (len(dims) - 1 - axis_at))
    return factor_of


def centred(rng, dims, spread, most, pieces=(), kind=jnp.bfloat16):
    drawn = jax.random.normal(rng, dims, jnp.float32) * spread
    if len(pieces) > 0:
        drawn = steps_of(rng, dims, pieces, -0.22, 0.18) * drawn
    return jnp.clip(drawn, min=-most, max=most).astype(kind)


def setup_inputs(seed: int = 0) -> dict:
    seeds = jax.random.split(jax.random.key(seed), 10)
    return {
        "features": centred(seeds[0], (N_COL, G, DIN), 1.0, 6.0, ((0, 64),), jnp.float32),
        "self_weight": centred(seeds[1], (DIN, DOUT), DIN ** -0.5, 0.5, (), jnp.float32),
        "neigh_weight": centred(seeds[2], (DIN, DOUT), DIN ** -0.5, 0.5, (), jnp.float32),
        "bias": centred(seeds[3], (DOUT,), 0.7, 4.0, (), jnp.float32),
        "edge_tiles": centred(seeds[4], (N_ROW, N_COL, STOPS * TS, TILE, TILE), (N_ROW * STOPS * TS * TILE // (2 * KT)) ** -0.5, 0.078125, ((0, 8), (1, 64))),
        "tile_rows": plant(jax.random.randint(seeds[5], (N_ROW, N_COL, STOPS * TS), 0, KT), jax.random.fold_in(seeds[5], 1), 0, KT - 1).astype(jnp.int32),
        "tile_cols": plant(jax.random.randint(seeds[6], (N_ROW, N_COL, STOPS * TS), 0, KT), jax.random.fold_in(seeds[6], 1), 0, KT - 1).astype(jnp.int32),
        "tile_count": draw_tile_count(jax.random.fold_in(seeds[9], 71), 0),
        "cotangent": centred(seeds[8], (N_COL, G, DOUT), 1.0, 6.0, ((0, 64), (1, 8)), jnp.float32),
    }


def layer(params, own, agg):
    self_weight, neigh_weight, bias = params
    pre = jnp.dot(own, self_weight, precision=lax.Precision.HIGHEST) + jnp.dot(agg, neigh_weight, precision=lax.Precision.HIGHEST) + bias
    hidden = jax.nn.gelu(pre, approximate=True)
    scale = lax.rsqrt(lax.optimization_barrier(jnp.mean(hidden * hidden, axis=-1, keepdims=True)) + 1e-06)
    return hidden * scale

def device_partial(r, c, features, edge_tiles, tile_rows, tile_cols, tile_count):
    tiles = edge_tiles[r, c].reshape(STOPS, TS, TILE, TILE)
    rows_idx = tile_rows[r, c].reshape(STOPS, TS)
    cols_idx = tile_cols[r, c].reshape(STOPS, TS)
    counts = tile_count[r, c]

    def one_stop(total, s):
        j = jnp.mod(c - r * STOPS - s, N_COL).astype(jnp.int32)
        block = features[j].reshape(KT, TILE, DIN)
        chosen = block[cols_idx[s]]
        live = (jnp.arange(TS, dtype=jnp.int32) < counts[s]).astype(jnp.float32)
        weights = tiles[s].astype(jnp.float32) * live[:, None, None]
        prod = jnp.einsum('tij,tjd->tid', weights, chosen, precision=lax.Precision.HIGHEST)
        return (total.at[rows_idx[s]].add(prod), None)
    start = jnp.zeros((KT, TILE, DIN), jnp.float32)
    total, _ = lax.scan(one_stop, start, jnp.arange(STOPS, dtype=jnp.int32))
    return total.reshape(G, DIN)

def reference(features, self_weight, neigh_weight, bias, edge_tiles, tile_rows, tile_cols, tile_count, cotangent):

    def block_sum(c):
        parts = jax.vmap(lambda r: device_partial(r, c, features, edge_tiles, tile_rows, tile_cols, tile_count))(jnp.arange(N_ROW, dtype=jnp.int32))
        return lax.optimization_barrier(jnp.sum(parts, axis=0))
    aggregate = lax.map(block_sum, jnp.arange(N_COL, dtype=jnp.int32))
    own = features.reshape(NODES, DIN)
    agg = aggregate.reshape(NODES, DIN)
    output, pullback = jax.vjp(lambda p: layer(p, own, agg), (self_weight, neigh_weight, bias))
    grads = pullback(cotangent.reshape(NODES, DOUT))[0]
    return (output.reshape(N_COL, G, DOUT), grads[0], grads[1], grads[2])
```

```python
import functools

import jax
import jax.numpy as jnp
from jax import lax
from jax.experimental import pallas as pl
from jax.experimental.pallas import tpu as pltpu
from jax.sharding import PartitionSpec as P

MESH = pl.DeviceIdType.MESH
TILE = 128
KT = 8
G = 1024
DIN = 128
DOUT = 256
STOPS = 8
TS = 12
NX, NY, NZ = 4, 8, 8
NC = 16
CR = G // NC
PACK = 8


class Place:
    def __init__(self):
        self.r = lax.axis_index("row")
        c = lax.axis_index("col")
        self.x = lax.div(self.r, 2)
        self.zh = lax.rem(self.r, 2)
        self.y = lax.div(c, 8)
        k = lax.rem(c, 8)
        self.zl = lax.div(k, 2)
        self.core = lax.rem(k, 2)
        self.z = self.zh * 4 + self.zl

    def dev(self, x=None, y=None, z=None, core=None):
        x = self.x if x is None else x
        y = self.y if y is None else y
        z = self.z if z is None else z
        core = self.core if core is None else core
        return (x * 2 + lax.div(z, 4), y * 8 + lax.rem(z, 4) * 2 + core)


def rows_of(ref, plane, i):
    return ref.at[plane, pl.ds(pl.multiple_of(i * CR, CR), CR)]


def remote(src, dst, send, recv, dev):
    return pltpu.make_async_remote_copy(
        src_ref=src, dst_ref=dst, send_sem=send, recv_sem=recv, device_id=dev, device_id_type=MESH
    )


def greet(devs):
    barrier = pltpu.get_barrier_semaphore()
    for dev in devs:
        pl.semaphore_signal(barrier, inc=1, device_id=dev, device_id_type=MESH)
    return barrier


def spread_kernel(feat, got, walk, y_send, y_recv, z_send, g_recv, s_send, s_recv, loc):
    me = Place()
    r, z, zl = me.r, me.z, me.zl
    fwd = me.dev(y=lax.rem(me.y + 1, NY))
    bwd = me.dev(y=lax.rem(me.y + NY - 1, NY))
    up = me.dev(z=lax.rem(z + 1, NZ))
    down = me.dev(z=lax.rem(z + NZ - 1, NZ))
    other = me.dev(core=1 - me.core)
    barrier = greet((fwd, bwd, up, down, other))
    load = pltpu.make_async_copy(feat.at[0], walk.at[0], loc.at[0])
    load.start()

    low_seam = (z == 3).astype(jnp.int32)
    high_seam = (z == 4).astype(jnp.int32)
    f_hops = jnp.minimum(r + 1 + low_seam, 7)
    b_hops = jnp.minimum(8 - r + high_seam, 7)
    f_most = jnp.minimum(2 * me.x + 2, 7)
    b_most = jnp.minimum(8 - 2 * me.x, 7)
    nf = lax.div(NC * b_most + lax.div(f_most + b_most, 2), f_most + b_most)
    h_up = lax.rem(r + 2 * low_seam, 8)
    h_down = lax.rem(r + 1 - 2 * high_seam, 8)
    h_other = lax.rem(r + me.core, 8)
    relays = jnp.logical_or(zl == 1, zl == 2)

    def y_copy(h_from, h_to, i, dev):
        return remote(rows_of(walk, h_from, i), rows_of(walk, h_to, i), y_send.at[h_to, i], y_recv.at[h_to, i], dev)

    def z_up(h, i):
        return remote(rows_of(walk, h, i), rows_of(got, 2, i), z_send.at[0, i], g_recv.at[0, i], up)

    def z_down(h, i):
        return remote(rows_of(walk, h, i), rows_of(got, 6, i), z_send.at[1, i], g_recv.at[2, i], down)

    def z_up_again(i):
        return remote(rows_of(got, 2, i), rows_of(got, 4, i), z_send.at[2, i], g_recv.at[1, i], up)

    def z_down_again(i):
        return remote(rows_of(got, 6, i), rows_of(got, 4, i), z_send.at[3, i], g_recv.at[1, i], down)

    def own_swap(h, i):
        return remote(rows_of(walk, h, i), rows_of(got, 1, i), s_send.at[0, i], s_recv.at[0, i], other)

    def swap(n, i):
        return remote(rows_of(got, 2 * n, i), rows_of(got, 2 * n + 1, i), s_send.at[n, i], s_recv.at[n, i], other)

    def use(h, i):
        @pl.when(h == h_up)
        def _():
            z_up(h, i).start()

        @pl.when(h == h_down)
        def _():
            z_down(h, i).start()

        @pl.when(h == h_other)
        def _():
            own_swap(h, i).start()

    load.wait()
    pl.semaphore_wait(barrier, 5)

    def z_first(i):
        z_up(0, i).wait_recv()

        @pl.when(relays)
        def _():
            z_up_again(i).start()

        swap(1, i).start()
        z_down(0, i).wait_recv()

        @pl.when(relays)
        def _():
            z_down_again(i).start()

        swap(3, i).start()

    def z_second(i):
        z_up_again(i).wait_recv()
        swap(2, i).start()

    def step(tau, carry):
        @pl.when(tau < nf)
        def _():
            y_copy(0, 1, tau, fwd).start()
            use(0, tau)

        @pl.when(nf + tau < NC)
        def _():
            y_copy(0, 7, nf + tau, bwd).start()
            use(0, nf + tau)

        def forward(h, carry):
            i = tau - h

            @pl.when(jnp.logical_and(i >= 0, i < nf))
            def _():
                y_copy(h - 1, h, i, fwd).wait_recv()

                @pl.when(h < f_hops)
                def _():
                    y_copy(h, h + 1, i, fwd).start()

                use(h, i)

            return carry

        lax.fori_loop(1, f_hops + 1, forward, 0)

        def backward(g, carry):
            i = nf + tau - g
            h = 8 - g

            @pl.when(jnp.logical_and(i >= nf, i < NC))
            def _():
                y_copy(h, h, i, bwd).wait_recv()

                @pl.when(g < b_hops)
                def _():
                    y_copy(h, h - 1, i, bwd).start()

                use(h, i)

            return carry

        lax.fori_loop(1, b_hops + 1, backward, 0)

        for lag, act in ((2, z_first), (4, z_second)):
            i = tau - f_most - lag

            @pl.when(jnp.logical_and(i >= 0, i < nf))
            def _():
                act(i)

            i2 = nf + tau - b_most - lag

            @pl.when(jnp.logical_and(i2 >= nf, i2 < NC))
            def _():
                act(i2)

        return carry

    steps = jnp.maximum(nf + f_most, NC - nf + b_most) + 4
    lax.fori_loop(0, steps, step, 0)
    keep = pltpu.make_async_copy(walk.at[r], got.at[0], loc.at[1])
    keep.start()

    def finish(i, carry):
        for n in range(4):
            swap(n, i).wait_recv() if n else own_swap(0, i).wait_recv()
            swap(n, i).wait_send() if n else own_swap(0, i).wait_send()
        z_up(0, i).wait_send()
        z_down(0, i).wait_send()

        @pl.when(relays)
        def _():
            z_up_again(i).wait_send()
            z_down_again(i).wait_send()

        @pl.when(i < nf)
        def _():
            def forward(h, carry):
                y_copy(h, h, i, fwd).wait_send()
                return carry

            lax.fori_loop(1, f_hops + 1, forward, 0)

        @pl.when(i >= nf)
        def _():
            def backward(g, carry):
                y_copy(8 - g, 8 - g, i, bwd).wait_send()
                return carry

            lax.fori_loop(1, b_hops + 1, backward, 0)

        return carry

    lax.fori_loop(0, NC, finish, 0)
    keep.wait()


def spread(features):
    dma = pltpu.SemaphoreType.DMA
    return pl.pallas_call(
        spread_kernel,
        out_shape=jax.ShapeDtypeStruct((8, G, DIN), jnp.float32),
        in_specs=[pl.BlockSpec(memory_space=pl.ANY)],
        out_specs=pl.BlockSpec(memory_space=pltpu.VMEM),
        scratch_shapes=[
            pltpu.VMEM((8, G, DIN), jnp.float32),
            dma((8, NC)),
            dma((8, NC)),
            dma((4, NC)),
            dma((3, NC)),
            dma((4, NC)),
            dma((4, NC)),
            dma((2,)),
        ],
        compiler_params=pltpu.CompilerParams(
            collective_id=0, has_side_effects=True, vmem_limit_bytes=20 * 2**20
        ),
        name="spread",
    )(features)


def products_kernel(rows, cols, counts, got, tiles, part):
    core = lax.rem(lax.axis_index("col"), 2)
    part[...] = jnp.zeros_like(part)

    def stop(s, carry):
        plane = jnp.where(jnp.logical_and(core == 0, lax.rem(s, 2) == 1), lax.rem(s + 2, 8), s)
        count = counts[0, 0, s]
        prods = []
        for t in range(TS):
            q = s * TS + t
            col = pl.multiple_of(cols[0, 0, q] * TILE, TILE)
            chosen = got[plane, pl.ds(col, TILE), :]
            chosen = jnp.where(t < count, chosen, 0.0)
            high = chosen.astype(jnp.bfloat16)
            low = (chosen - high.astype(jnp.float32)).astype(jnp.bfloat16)
            both = jnp.dot(
                tiles[0, 0, q], jnp.concatenate([high, low], axis=1), preferred_element_type=jnp.float32
            )
            prods.append(both[:, :DIN] + both[:, DIN:])
        for t in range(TS):
            at = pl.ds(pl.multiple_of(rows[0, 0, s * TS + t] * TILE, TILE), TILE)
            part[at, :] = part[at, :] + prods[t]
        return carry

    lax.fori_loop(0, STOPS, stop, 0)


def products(rows, cols, counts, got, tiles):
    smem = pl.BlockSpec(memory_space=pltpu.SMEM)
    vmem = pl.BlockSpec(memory_space=pltpu.VMEM)
    return pl.pallas_call(
        products_kernel,
        out_shape=jax.ShapeDtypeStruct((G, DIN), jnp.float32),
        in_specs=[smem, smem, smem, vmem, vmem],
        out_specs=vmem,
        compiler_params=pltpu.CompilerParams(vmem_limit_bytes=20 * 2**20),
        name="products",
    )(rows, cols, counts, got, tiles)


def exact(a, b, dims=((1,), (0,))):
    return lax.dot_general(
        a, b, (dims, ((), ())), precision=lax.Precision.HIGHEST, preferred_element_type=jnp.float32
    )


def finish_kernel(
    part,
    feat,
    w_self,
    w_neigh,
    bias,
    cot,
    out,
    g_self,
    g_neigh,
    g_bias,
    own,
    rs_in,
    half_in,
    half_out,
    packs,
    pack_in,
    xs,
    ys,
    zs,
    mine,
    loc,
    rs_send,
    rs_recv,
    h_send,
    h_recv,
    c_send,
    c_recv,
    x_send,
    x_recv,
    y_send,
    y_recv,
    z_send,
    z_recv,
):
    me = Place()
    r, x, y, z, core = me.r, me.x, me.y, me.z, me.core
    x_dev = [me.dev(x=lax.rem(x + d, NX)) for d in range(NX)]
    y_dev = [me.dev(y=lax.rem(y + d, NY)) for d in range(NY)]
    z_dev = [me.dev(z=lax.rem(z + d, NZ)) for d in range(NZ)]
    other = me.dev(core=1 - core)
    barrier = greet(x_dev[1:] + y_dev[1:] + z_dev[1:] + [other])
    load = pltpu.make_async_copy(feat.at[0, pl.ds(pl.multiple_of(r * TILE, TILE), TILE)], own, loc)
    load.start()
    pl.semaphore_wait(barrier, NX + NY + NZ - 2)

    def to_x(d):
        there = lax.rem(x + d, NX)
        return remote(
            part.at[pl.ds(pl.multiple_of(there * 2 * TILE, 2 * TILE), 2 * TILE)],
            rs_in.at[d - 1],
            rs_send.at[d - 1],
            rs_recv.at[d - 1],
            x_dev[d],
        )

    for d in (2, 1, 3):
        to_x(d).start()
    for d in (1, 3, 2):
        to_x(d).wait_recv()

    def summed(h):
        at = pl.ds(pl.multiple_of(h * TILE, TILE), TILE)
        mine_at = pl.ds(pl.multiple_of((2 * x + h) * TILE, TILE), TILE)
        return part[mine_at, :] + rs_in[0, at, :] + rs_in[1, at, :] + rs_in[2, at, :]

    half_out[...] = summed(1 - me.zh)
    over = remote(half_out, half_in, h_send, h_recv, z_dev[4])
    over.start()
    kept = summed(me.zh)
    load.wait()
    mine_rows = own[...]
    start = exact(mine_rows, w_self[...]) + bias[...]
    over.wait_recv()
    agg = kept + half_in[...]

    v = start + exact(agg, w_neigh[...])
    a = 0.7978845608028654
    b = 0.044715
    t = jnp.tanh(a * (v + b * (v * v * v)))
    hidden = 0.5 * v * (1.0 + t)
    scale = lax.rsqrt(jnp.mean(hidden * hidden, axis=-1, keepdims=True) + 1e-06)
    out[0] = hidden * scale
    g = cot[0]
    dot = jnp.mean(g * hidden, axis=-1, keepdims=True)
    d_hidden = scale * (g - hidden * (scale * scale * dot))
    slope = 0.5 * (1.0 + t) + 0.5 * v * (1.0 - t * t) * (a * (1.0 + 3.0 * b * (v * v)))
    d_pre = d_hidden * slope
    gs = exact(mine_rows, d_pre, ((0,), (0,)))
    gn = exact(agg, d_pre, ((0,), (0,)))
    gb = jnp.sum(d_pre, axis=0, keepdims=True)

    packs[0, 0:128, :] = gs[:, :128]
    packs[0, 128:256, :] = gs[:, 128:]
    packs[1, 0:128, :] = gn[:, :128]
    packs[1, 128:256, :] = gn[:, 128:]
    first = jnp.broadcast_to(gb[:, :128], (PACK, 128))
    second = jnp.broadcast_to(gb[:, 128:], (PACK, 128))
    gbp = jnp.where(lax.broadcasted_iota(jnp.int32, (PACK, 128), 0) == 0, first, second)
    packs[0, 256:264, :] = gbp
    packs[1, 256:264, :] = gbp
    core_swap = remote(packs.at[1 - core], pack_in, c_send.at[0], c_recv.at[0], other)
    core_swap.start()
    core_swap.wait_recv()
    b_now = gbp + pack_in[256:264, :]

    def piece(n, size):
        at = pl.ds(pl.multiple_of(n * size, size), size)
        return packs[core, at, :] + pack_in[at, :]

    for n in range(NX):
        xs[0, n, 0:64, :] = piece(n, 64)
        xs[0, n, 64:72, :] = b_now

    def x_copy(d):
        return remote(
            xs.at[0, lax.rem(x + d, NX)], xs.at[1, x], x_send.at[0, d], x_recv.at[0, x], x_dev[d]
        )

    def x_wait(d):
        src = lax.rem(x + NX - d, NX)
        remote(xs.at[0, 0], xs.at[1, src], x_send.at[0, d], x_recv.at[0, src], x_dev[d]).wait_recv()

    for d in (2, 1, 3):
        x_copy(d).start()
    xs[1, x] = xs[0, x]
    for d in (1, 3, 2):
        x_wait(d)
    x_sum = xs[1, 0] + xs[1, 1] + xs[1, 2] + xs[1, 3]

    for n in range(NY):
        ys[0, n, 0:8, :] = x_sum[n * 8 : n * 8 + 8]
        ys[0, n, 8:16, :] = x_sum[64:72]

    def y_copy(d):
        return remote(
            ys.at[0, lax.rem(y + d, NY)], ys.at[1, y], y_send.at[0, d], y_recv.at[0, y], y_dev[d]
        )

    def y_wait(d):
        src = lax.rem(y + NY - d, NY)
        remote(ys.at[0, 0], ys.at[1, src], y_send.at[0, d], y_recv.at[0, src], y_dev[d]).wait_recv()

    order = (4, 3, 5, 2, 6, 1, 7)
    for d in order:
        y_copy(d).start()
    ys[1, y] = ys[0, y]
    for d in order[::-1]:
        y_wait(d)
    y_sum = ys[1, 0]
    for n in range(1, NY):
        y_sum = y_sum + ys[1, n]

    zs[0] = y_sum
    zs[1 + z] = y_sum

    def z_copy(d):
        return remote(zs.at[0], zs.at[1 + z], z_send.at[d], z_recv.at[z], z_dev[d])

    def z_wait(d):
        src = lax.rem(z + NZ - d, NZ)
        remote(zs.at[0], zs.at[1 + src], z_send.at[d], z_recv.at[src], z_dev[d]).wait_recv()

    for d in order:
        z_copy(d).start()
    for d in order[::-1]:
        z_wait(d)
    z_sum = zs[1]
    for n in range(1, NZ):
        z_sum = z_sum + zs[1 + n]
    g_bias[:, 0:128] = z_sum[8:9]
    g_bias[:, 128:256] = z_sum[9:10]

    def at_y(n):
        return mine.at[core, pl.ds(pl.multiple_of(x * 64 + n * 8, 8), 8)]

    def y_back(d):
        return remote(at_y(y), at_y(y), y_send.at[1, d], y_recv.at[1, y], y_dev[d])

    def y_back_wait(d):
        src = lax.rem(y + NY - d, NY)
        remote(at_y(src), at_y(src), y_send.at[1, d], y_recv.at[1, src], y_dev[d]).wait_recv()

    mine[core, pl.ds(pl.multiple_of(x * 64 + y * 8, 8), 8), :] = z_sum[0:8]
    for d in order:
        y_back(d).start()
    for d in order[::-1]:
        y_back_wait(d)

    def at_x(n):
        return mine.at[core, pl.ds(pl.multiple_of(n * 64, 64), 64)]

    def x_back(d):
        return remote(at_x(x), at_x(x), x_send.at[1, d], x_recv.at[1, x], x_dev[d])

    def x_back_wait(d):
        src = lax.rem(x + NX - d, NX)
        remote(at_x(src), at_x(src), x_send.at[1, d], x_recv.at[1, src], x_dev[d]).wait_recv()

    for d in (2, 1, 3):
        x_back(d).start()
    for d in (1, 3, 2):
        x_back_wait(d)
    core_back = remote(mine.at[core], mine.at[core], c_send.at[1], c_recv.at[1], other)
    core_back_in = remote(mine.at[1 - core], mine.at[1 - core], c_send.at[1], c_recv.at[1], other)
    core_back.start()
    core_back_in.wait_recv()
    g_self[:, 0:128] = mine[0, 0:128]
    g_self[:, 128:256] = mine[0, 128:256]
    g_neigh[:, 0:128] = mine[1, 0:128]
    g_neigh[:, 128:256] = mine[1, 128:256]

    for d in (1, 2, 3):
        to_x(d).wait_send()
        x_copy(d).wait_send()
        x_back(d).wait_send()
    over.wait_send()
    core_swap.wait_send()
    core_back.wait_send()
    for d in range(1, 8):
        y_copy(d).wait_send()
        z_copy(d).wait_send()
        y_back(d).wait_send()


def finish(part, features, w_self, w_neigh, bias, cotangent):
    dma = pltpu.SemaphoreType.DMA
    vmem = pl.BlockSpec(memory_space=pltpu.VMEM)
    f32 = jnp.float32
    return pl.pallas_call(
        finish_kernel,
        out_shape=(
            jax.ShapeDtypeStruct((1, TILE, DOUT), f32),
            jax.ShapeDtypeStruct((DIN, DOUT), f32),
            jax.ShapeDtypeStruct((DIN, DOUT), f32),
            jax.ShapeDtypeStruct((1, DOUT), f32),
        ),
        in_specs=[vmem, pl.BlockSpec(memory_space=pl.ANY), vmem, vmem, vmem, vmem],
        out_specs=(vmem, vmem, vmem, vmem),
        scratch_shapes=[
            pltpu.VMEM((TILE, DIN), f32),
            pltpu.VMEM((3, 2 * TILE, DIN), f32),
            pltpu.VMEM((TILE, DIN), f32),
            pltpu.VMEM((TILE, DIN), f32),
            pltpu.VMEM((2, 264, 128), f32),
            pltpu.VMEM((264, 128), f32),
            pltpu.VMEM((2, NX, 72, 128), f32),
            pltpu.VMEM((2, NY, 16, 128), f32),
            pltpu.VMEM((1 + NZ, 16, 128), f32),
            pltpu.VMEM((2, 256, 128), f32),
            dma(()),
            dma((3,)),
            dma((3,)),
            dma(()),
            dma(()),
            dma((2,)),
            dma((2,)),
            dma((2, NX)),
            dma((2, NX)),
            dma((2, NY)),
            dma((2, NY)),
            dma((NZ,)),
            dma((NZ,)),
        ],
        compiler_params=pltpu.CompilerParams(
            collective_id=1, has_side_effects=True, vmem_limit_bytes=20 * 2**20
        ),
        name="finish",
    )(part, features, w_self, w_neigh, bias, cotangent)


def on_device(
    features, self_weight, neigh_weight, bias, edge_tiles, tile_rows, tile_cols, tile_count, cotangent
):
    got = spread(features)
    part = products(tile_rows, tile_cols, tile_count, got, edge_tiles)
    out, gs, gn, gb = finish(part, features, self_weight, neigh_weight, bias.reshape(1, DOUT), cotangent)
    return out, gs, gn, gb.reshape(DOUT)


def solution(mesh):
    in_specs = (
        P("col", None, None),
        P(),
        P(),
        P(),
        P("row", "col", None, None, None),
        P("row", "col", None),
        P("row", "col", None),
        P("row", "col", None),
        P("col", "row", None),
    )
    out_specs = (P("col", "row", None), P(), P(), P())
    return jax.shard_map(on_device, mesh=mesh, in_specs=in_specs, out_specs=out_specs, check_vma=False)
```

```python
import jax
import jax.numpy as jnp
from jax import lax
from jax.experimental import pallas as pl
from jax.experimental.pallas import tpu as pltpu
from jax.sharding import PartitionSpec as P

MESH = pl.DeviceIdType.MESH
TILE = 128
KT = 8
G = 1024
DIN = 128
DOUT = 256
STOPS = 8
TS = 12
NX, NY, NZ = 4, 8, 8
PR = G // NX
NS = 4
PART = PR // NS
PACK = 8


class Place:
    def __init__(self):
        self.r = lax.axis_index("row")
        c = lax.axis_index("col")
        self.x = lax.div(self.r, 2)
        self.zh = lax.rem(self.r, 2)
        self.y = lax.div(c, 8)
        k = lax.rem(c, 8)
        self.zl = lax.div(k, 2)
        self.core = lax.rem(k, 2)
        self.z = self.zh * 4 + self.zl

    def dev(self, x=None, y=None, z=None, core=None):
        x = self.x if x is None else x
        y = self.y if y is None else y
        z = self.z if z is None else z
        core = self.core if core is None else core
        return (x * 2 + lax.div(z, 4), y * 8 + lax.rem(z, 4) * 2 + core)


def rows_of(ref, plane, p, rows=PR):
    return ref.at[plane, pl.ds(pl.multiple_of(p * rows, rows), rows)]


def remote(src, dst, send, recv, dev):
    return pltpu.make_async_remote_copy(
        src_ref=src, dst_ref=dst, send_sem=send, recv_sem=recv, device_id=dev, device_id_type=MESH
    )


def greet(devs):
    barrier = pltpu.get_barrier_semaphore()
    for dev in devs:
        pl.semaphore_signal(barrier, inc=1, device_id=dev, device_id_type=MESH)
    return barrier


def spread_kernel(
    feat,
    got,
    walk,
    walk2,
    b_buf,
    y_send,
    y_recv,
    w_send,
    w_recv,
    x_send,
    ab_recv,
    x2_send,
    seam_send,
    z_send,
    g_recv,
    s_send,
    s_recv,
    loc,
):
    me = Place()
    x, z, zl, zh, core = me.x, me.z, me.zl, me.zh, me.core
    y_at = {d: me.dev(y=lax.rem(me.y + d, NY)) for d in (1, 2, 6, 7)}
    z_at = {d: me.dev(z=lax.rem(z + d, NZ)) for d in (1, 2, 6, 7)}
    x_at = [me.dev(x=lax.rem(x + d, NX)) for d in range(NX)]
    other = me.dev(core=1 - core)
    low_seam = z == 3
    high_seam = z == 4
    seam = jnp.logical_or(low_seam, high_seam)
    far = jnp.where(low_seam, 4, 3)
    barrier = greet(list(y_at.values()) + list(z_at.values()) + x_at[1:] + [other])

    @pl.when(seam)
    def _():
        greet([me.dev(x=lax.rem(x + d, NX), z=far) for d in range(1, NX)])

    load = pltpu.make_async_copy(feat.at[0, pl.ds(pl.multiple_of(x * PR, PR), PR)], walk.at[0], loc)
    load.start()
    load.wait()
    pl.semaphore_wait(barrier, 12 + 3 * seam.astype(jnp.int32))

    def y_copy(src, dst, d):
        return remote(walk.at[src], walk.at[dst], y_send.at[dst], y_recv.at[dst, 0], y_at[d])

    def y_part(src, dst, d, s):
        at = pl.ds(s * PART, PART)
        return remote(walk.at[src, at], walk.at[dst, at], y_send.at[dst], y_recv.at[dst, s], y_at[d])

    half = PR // 2

    def piece(plane, p, j=None):
        ref = b_buf if plane == 1 else got.at[plane]
        if j is None:
            return ref.at[pl.ds(pl.multiple_of(p * PR, PR), PR)]
        return ref.at[pl.ds(pl.multiple_of(p * PR + j * half, half), half)]

    def walked(h, j):
        return walk.at[h] if j is None else walk.at[h, pl.ds(j * half, half)]

    def x_copy(h, v, j):
        to = h // 2 if v == 0 else lax.rem(h // 2 - zh + NX, NX)
        dev = me.dev(x=jnp.int32(to))
        return to, remote(walked(h, j), piece(v, x, j), x_send.at[h], ab_recv.at[v, x, j or 0], dev)

    def seam_copy(h, low, j):
        to = lax.rem(jnp.int32(h // 2 + (NX - 1 if low else 0)), NX)
        plane = 2 if low else 6
        side = 0 if low else 1
        dev = me.dev(x=to, z=jnp.int32(4 if low else 3))
        return remote(walked(h, j), piece(plane, x, j), seam_send.at[h], g_recv.at[side, x], dev)

    def across(h, j=None, finish=False):
        for v in (0, 1):
            fits = zh == h % 2 if v == 0 else zh != h % 2

            @pl.when(fits)
            def _():
                to, copy = x_copy(h, v, j)

                @pl.when(to != x)
                def _():
                    copy.wait_send() if finish else copy.start()

                if not finish:

                    @pl.when(to == x)
                    def _():
                        pltpu.make_async_copy(walked(h, j), piece(v, x, j), ab_recv.at[v, x, j]).start()

        if h % 2 == 0:
            for low, fits in ((True, low_seam), (False, high_seam)):

                @pl.when(fits)
                def _():
                    copy = seam_copy(h, low, j)
                    copy.wait_send() if finish else copy.start()

    def up_copy(p, j=None):
        return remote(piece(0, p, j), piece(2, p, j), z_send.at[0, p], g_recv.at[0, p], z_at[1])

    def down_copy(p, j=None):
        return remote(piece(1, p, j), piece(6, p, j), z_send.at[1, p], g_recv.at[1, p], z_at[7])

    def own_swap(v, p):
        return remote(piece(v, p), rows_of(got, 1, p), s_send.at[0], s_recv.at[0], other)

    def swap(n, p):
        return remote(rows_of(got, 2 * n, p), rows_of(got, 2 * n + 1, p), s_send.at[n], s_recv.at[n], other)

    def swapped(n):
        return remote(got.at[2 * n], got.at[2 * n + 1], s_send.at[n], s_recv.at[n], other)

    def pass_on(v):
        for j in range(2):
            for p in range(NX):
                remote(walked(0, j), piece(v, p, j), x_send.at[0], ab_recv.at[v, p, j], other).wait_recv()

                @pl.when(jnp.logical_not(low_seam if v == 0 else high_seam))
                def _():
                    (up_copy(p, j) if v == 0 else down_copy(p, j)).start()

                if j == 1:

                    @pl.when(core == v)
                    def _():
                        own_swap(v, p).start()

    near_a = jnp.minimum(me.r, 8 - me.r)
    next_r = lax.rem(me.r + 1, 8)
    near_b = jnp.minimum(next_r, 8 - next_r)

    def pass_near(n):
        for v, near in ((0, near_a), (1, near_b)):

            @pl.when(near == n)
            def _():
                pass_on(v)

    even = jnp.logical_xor(zl >= 2, zh == 1)
    two = jnp.where(core == 0, 2, 6)
    ahead = remote(walk.at[0], walk2.at[0], w_send.at[0], w_recv.at[0], me.dev(z=lax.rem(z + two, NZ)))
    def w_copy(src, dst, d):
        return remote(walk2.at[src], walk2.at[dst], w_send.at[dst], w_recv.at[dst], y_at[d])

    def w_half(src, dst, d, n):
        at = pl.ds(n * half, half)
        sem = dst if n == 0 else 8
        return remote(walk2.at[src, at], walk2.at[dst, at], w_send.at[sem], w_recv.at[sem], y_at[d])

    def across2(h, finish=False):
        to = jnp.where(zl >= 2, h // 2, lax.rem(h // 2 - zh + NX, NX))
        copy = remote(walk2.at[h], rows_of(got, 4, x), x2_send.at[h], g_recv.at[2, x], me.dev(x=to))

        @pl.when(to != x)
        def _():
            copy.wait_send() if finish else copy.start()

        if not finish:

            @pl.when(to == x)
            def _():
                pltpu.make_async_copy(walk2.at[h], rows_of(got, 4, x), g_recv.at[2, x]).start()

    def w_start():
        ahead.wait_recv()

        @pl.when(even)
        def _():
            w_copy(0, 2, 2).start()
            w_copy(0, 6, 6).start()
            across2(0)

        @pl.when(jnp.logical_not(even))
        def _():
            w_copy(0, 1, 1).start()
            w_copy(0, 7, 7).start()

    def w_near():
        @pl.when(even)
        def _():
            w_copy(2, 2, 2).wait_recv()
            w_half(2, 4, 2, 0).start()
            w_copy(6, 6, 6).wait_recv()
            w_half(6, 4, 6, 1).start()
            across2(2)
            across2(6)

        @pl.when(jnp.logical_not(even))
        def _():
            w_copy(1, 1, 1).wait_recv()
            w_copy(1, 3, 2).start()
            w_copy(7, 7, 7).wait_recv()
            w_copy(7, 5, 6).start()
            across2(1)
            across2(7)

    def w_far():
        @pl.when(even)
        def _():
            w_half(2, 4, 2, 0).wait_recv()
            w_half(6, 4, 6, 1).wait_recv()
            across2(4)

        @pl.when(jnp.logical_not(even))
        def _():
            w_copy(3, 3, 2).wait_recv()
            across2(3)
            w_copy(5, 5, 6).wait_recv()
            across2(5)

    for s in range(NS):
        y_part(0, 1, 1, s).start()
        y_part(0, 7, 7, s).start()
    ahead.start()
    across(0, 0)
    across(0, 1)
    for n in range(1, 5):
        for s in range(NS):
            first = s < NS // 2
            if n < 4 or first:
                y_part(n, n, 1, s).wait_recv()
            if n < 3 or (n == 3 and first):
                y_part(n, n + 1, 1, s).start()
            if n < 4 or not first:
                y_part(8 - n, 8 - n, 7, s).wait_recv()
            if n < 3 or (n == 3 and not first):
                y_part(8 - n, 7 - n, 7, s).start()
            if s % (NS // 2) == NS // 2 - 1 and n < 4:
                across(n, s // (NS // 2))
                across(8 - n, s // (NS // 2))
        if n == 4:
            across(4, 0)
            across(4, 1)
        if n == 3:
            w_start()
        if n >= 2:
            pass_near(n - 2)
    w_near()
    pass_near(3)
    pass_near(4)
    w_far()

    for p in range(NX):
        up_copy(p).wait_recv()
        swap(1, p).start()
        down_copy(p).wait_recv()
        swap(3, p).start()
    for p in range(NX):
        remote(walk.at[0], rows_of(got, 4, p), x2_send.at[0], g_recv.at[2, p], other).wait_recv()
        swap(2, p).start()

    for n in (0, 1, 3, 2):
        swapped(n).wait_recv()
        swapped(n).wait_send()
    for p in range(NX):

        @pl.when(jnp.logical_not(low_seam))
        def _():
            up_copy(p).wait_send()

        @pl.when(jnp.logical_not(high_seam))
        def _():
            down_copy(p).wait_send()

    for h in range(8):
        across(h, finish=True)
        if h:
            y_copy(h, h, 1).wait_send()
    ahead.wait_send()

    @pl.when(even)
    def _():
        for h in (0, 2, 4, 6):
            across2(h, finish=True)
        w_copy(2, 2, 2).wait_send()
        w_copy(6, 6, 6).wait_send()
        w_half(2, 4, 2, 0).wait_send()
        w_half(6, 4, 6, 1).wait_send()

    @pl.when(jnp.logical_not(even))
    def _():
        for h in (1, 3, 5, 7):
            across2(h, finish=True)
            w_copy(h, h, 1).wait_send()


def spread(features):
    dma = pltpu.SemaphoreType.DMA
    return pl.pallas_call(
        spread_kernel,
        out_shape=jax.ShapeDtypeStruct((8, G, DIN), jnp.float32),
        in_specs=[pl.BlockSpec(memory_space=pltpu.HBM)],
        out_specs=pl.BlockSpec(memory_space=pltpu.VMEM),
        scratch_shapes=[
            pltpu.VMEM((8, PR, DIN), jnp.float32),
            pltpu.VMEM((8, PR, DIN), jnp.float32),
            pltpu.VMEM((G, DIN), jnp.float32),
            dma((8,)),
            dma((8, NS)),
            dma((9,)),
            dma((9,)),
            dma((8,)),
            dma((2, NX, 2)),
            dma((8,)),
            dma((8,)),
            dma((2, NX)),
            dma((3, NX)),
            dma((4,)),
            dma((4,)),
            dma(()),
        ],
        compiler_params=pltpu.CompilerParams(
            collective_id=0, has_side_effects=True, vmem_limit_bytes=20 * 2**20
        ),
        name="spread",
    )(features)


def products_kernel(rows, cols, counts, got, tiles, part):
    core = lax.rem(lax.axis_index("col"), 2)
    part[...] = jnp.zeros_like(part)

    def stop(s, carry):
        plane = jnp.where(jnp.logical_and(core == 0, lax.rem(s, 2) == 1), lax.rem(s + 2, 8), s)
        count = counts[0, 0, s]
        prods = []
        for t in range(TS):
            q = s * TS + t
            col = pl.multiple_of(cols[0, 0, q] * TILE, TILE)
            chosen = got[plane, pl.ds(col, TILE), :]
            chosen = jnp.where(t < count, chosen, 0.0)
            high = chosen.astype(jnp.bfloat16)
            low = (chosen - high.astype(jnp.float32)).astype(jnp.bfloat16)
            both = jnp.dot(
                tiles[0, 0, q], jnp.concatenate([high, low], axis=1), preferred_element_type=jnp.float32
            )
            prods.append(both[:, :DIN] + both[:, DIN:])
        for t in range(TS):
            at = pl.ds(pl.multiple_of(rows[0, 0, s * TS + t] * TILE, TILE), TILE)
            part[at, :] = part[at, :] + prods[t]
        return carry

    lax.fori_loop(0, STOPS, stop, 0)


def products(rows, cols, counts, got, tiles):
    smem = pl.BlockSpec(memory_space=pltpu.SMEM)
    vmem = pl.BlockSpec(memory_space=pltpu.VMEM)
    return pl.pallas_call(
        products_kernel,
        out_shape=jax.ShapeDtypeStruct((G, DIN), jnp.float32),
        in_specs=[smem, smem, smem, vmem, vmem],
        out_specs=vmem,
        compiler_params=pltpu.CompilerParams(vmem_limit_bytes=20 * 2**20),
        name="products",
    )(rows, cols, counts, got, tiles)


def exact(a, b, dims=((1,), (0,))):
    return lax.dot_general(
        a, b, (dims, ((), ())), precision=lax.Precision.HIGHEST, preferred_element_type=jnp.float32
    )


def finish_kernel(
    part,
    feat,
    w_self,
    w_neigh,
    bias,
    cot,
    out,
    g_self,
    g_neigh,
    g_bias,
    own,
    rs_in,
    half_in,
    half_out,
    packs,
    pack_in,
    xs,
    ys,
    zs,
    mine,
    loc,
    rs_send,
    rs_recv,
    h_send,
    h_recv,
    c_send,
    c_recv,
    x_send,
    x_recv,
    y_send,
    y_recv,
    z_send,
    z_recv,
):
    me = Place()
    r, x, y, z, core = me.r, me.x, me.y, me.z, me.core
    x_dev = [me.dev(x=lax.rem(x + d, NX)) for d in range(NX)]
    y_dev = [me.dev(y=lax.rem(y + d, NY)) for d in range(NY)]
    z_dev = [me.dev(z=lax.rem(z + d, NZ)) for d in range(NZ)]
    other = me.dev(core=1 - core)
    barrier = greet(x_dev[1:] + y_dev[1:] + z_dev[1:] + [other])
    load = pltpu.make_async_copy(feat.at[0, pl.ds(pl.multiple_of(r * TILE, TILE), TILE)], own, loc)
    load.start()
    pl.semaphore_wait(barrier, NX + NY + NZ - 2)

    def to_x(d):
        there = lax.rem(x + d, NX)
        return remote(
            part.at[pl.ds(pl.multiple_of(there * 2 * TILE, 2 * TILE), 2 * TILE)],
            rs_in.at[d - 1],
            rs_send.at[d - 1],
            rs_recv.at[d - 1],
            x_dev[d],
        )

    for d in (2, 1, 3):
        to_x(d).start()
    for d in (1, 3, 2):
        to_x(d).wait_recv()

    def summed(h):
        at = pl.ds(pl.multiple_of(h * TILE, TILE), TILE)
        mine_at = pl.ds(pl.multiple_of((2 * x + h) * TILE, TILE), TILE)
        return part[mine_at, :] + rs_in[0, at, :] + rs_in[1, at, :] + rs_in[2, at, :]

    half_out[...] = summed(1 - me.zh)
    over = remote(half_out, half_in, h_send, h_recv, z_dev[4])
    over.start()
    kept = summed(me.zh)
    load.wait()
    mine_rows = own[...]
    start = exact(mine_rows, w_self[...]) + bias[...]
    over.wait_recv()
    agg = kept + half_in[...]

    v = start + exact(agg, w_neigh[...])
    a = 0.7978845608028654
    b = 0.044715
    t = jnp.tanh(a * (v + b * (v * v * v)))
    hidden = 0.5 * v * (1.0 + t)
    scale = lax.rsqrt(jnp.mean(hidden * hidden, axis=-1, keepdims=True) + 1e-06)
    out[0] = hidden * scale
    g = cot[0]
    dot = jnp.mean(g * hidden, axis=-1, keepdims=True)
    d_hidden = scale * (g - hidden * (scale * scale * dot))
    slope = 0.5 * (1.0 + t) + 0.5 * v * (1.0 - t * t) * (a * (1.0 + 3.0 * b * (v * v)))
    d_pre = d_hidden * slope
    gs = exact(mine_rows, d_pre, ((0,), (0,)))
    gn = exact(agg, d_pre, ((0,), (0,)))
    gb = jnp.sum(d_pre, axis=0, keepdims=True)

    packs[0, 0:128, :] = gs[:, :128]
    packs[0, 128:256, :] = gs[:, 128:]
    packs[1, 0:128, :] = gn[:, :128]
    packs[1, 128:256, :] = gn[:, 128:]
    first = jnp.broadcast_to(gb[:, :128], (PACK, 128))
    second = jnp.broadcast_to(gb[:, 128:], (PACK, 128))
    gbp = jnp.where(lax.broadcasted_iota(jnp.int32, (PACK, 128), 0) == 0, first, second)
    packs[0, 256:264, :] = gbp
    packs[1, 256:264, :] = gbp
    core_swap = remote(packs.at[1 - core], pack_in, c_send.at[0], c_recv.at[0], other)
    core_swap.start()
    core_swap.wait_recv()
    b_now = gbp + pack_in[256:264, :]

    def piece(n, size):
        at = pl.ds(pl.multiple_of(n * size, size), size)
        return packs[core, at, :] + pack_in[at, :]

    for n in range(NX):
        xs[0, n, 0:64, :] = piece(n, 64)
        xs[0, n, 64:72, :] = b_now

    def x_copy(d):
        return remote(
            xs.at[0, lax.rem(x + d, NX)], xs.at[1, x], x_send.at[0, d], x_recv.at[0, x], x_dev[d]
        )

    def x_wait(d):
        src = lax.rem(x + NX - d, NX)
        remote(xs.at[0, 0], xs.at[1, src], x_send.at[0, d], x_recv.at[0, src], x_dev[d]).wait_recv()

    for d in (2, 1, 3):
        x_copy(d).start()
    xs[1, x] = xs[0, x]
    for d in (1, 3, 2):
        x_wait(d)
    x_sum = xs[1, 0] + xs[1, 1] + xs[1, 2] + xs[1, 3]

    for n in range(NY):
        ys[0, n, 0:8, :] = x_sum[n * 8 : n * 8 + 8]
        ys[0, n, 8:16, :] = x_sum[64:72]

    def y_copy(d):
        return remote(
            ys.at[0, lax.rem(y + d, NY)], ys.at[1, y], y_send.at[0, d], y_recv.at[0, y], y_dev[d]
        )

    def y_wait(d):
        src = lax.rem(y + NY - d, NY)
        remote(ys.at[0, 0], ys.at[1, src], y_send.at[0, d], y_recv.at[0, src], y_dev[d]).wait_recv()

    order = (4, 3, 5, 2, 6, 1, 7)
    for d in order:
        y_copy(d).start()
    ys[1, y] = ys[0, y]
    for d in order[::-1]:
        y_wait(d)
    y_sum = ys[1, 0]
    for n in range(1, NY):
        y_sum = y_sum + ys[1, n]

    zs[0] = y_sum
    zs[1 + z] = y_sum

    def z_copy(d):
        return remote(zs.at[0], zs.at[1 + z], z_send.at[d], z_recv.at[z], z_dev[d])

    def z_wait(d):
        src = lax.rem(z + NZ - d, NZ)
        remote(zs.at[0], zs.at[1 + src], z_send.at[d], z_recv.at[src], z_dev[d]).wait_recv()

    for d in order:
        z_copy(d).start()
    for d in order[::-1]:
        z_wait(d)
    z_sum = zs[1]
    for n in range(1, NZ):
        z_sum = z_sum + zs[1 + n]
    g_bias[:, 0:128] = z_sum[8:9]
    g_bias[:, 128:256] = z_sum[9:10]

    def at_y(n):
        return mine.at[core, pl.ds(pl.multiple_of(x * 64 + n * 8, 8), 8)]

    def y_back(d):
        return remote(at_y(y), at_y(y), y_send.at[1, d], y_recv.at[1, y], y_dev[d])

    def y_back_wait(d):
        src = lax.rem(y + NY - d, NY)
        remote(at_y(src), at_y(src), y_send.at[1, d], y_recv.at[1, src], y_dev[d]).wait_recv()

    mine[core, pl.ds(pl.multiple_of(x * 64 + y * 8, 8), 8), :] = z_sum[0:8]
    for d in order:
        y_back(d).start()
    for d in order[::-1]:
        y_back_wait(d)

    def at_x(n):
        return mine.at[core, pl.ds(pl.multiple_of(n * 64, 64), 64)]

    def x_back(d):
        return remote(at_x(x), at_x(x), x_send.at[1, d], x_recv.at[1, x], x_dev[d])

    def x_back_wait(d):
        src = lax.rem(x + NX - d, NX)
        remote(at_x(src), at_x(src), x_send.at[1, d], x_recv.at[1, src], x_dev[d]).wait_recv()

    for d in (2, 1, 3):
        x_back(d).start()
    for d in (1, 3, 2):
        x_back_wait(d)
    core_back = remote(mine.at[core], mine.at[core], c_send.at[1], c_recv.at[1], other)
    core_back_in = remote(mine.at[1 - core], mine.at[1 - core], c_send.at[1], c_recv.at[1], other)
    core_back.start()
    core_back_in.wait_recv()
    g_self[:, 0:128] = mine[0, 0:128]
    g_self[:, 128:256] = mine[0, 128:256]
    g_neigh[:, 0:128] = mine[1, 0:128]
    g_neigh[:, 128:256] = mine[1, 128:256]

    for d in (1, 2, 3):
        to_x(d).wait_send()
        x_copy(d).wait_send()
        x_back(d).wait_send()
    over.wait_send()
    core_swap.wait_send()
    core_back.wait_send()
    for d in range(1, 8):
        y_copy(d).wait_send()
        z_copy(d).wait_send()
        y_back(d).wait_send()


def finish(part, features, w_self, w_neigh, bias, cotangent):
    dma = pltpu.SemaphoreType.DMA
    vmem = pl.BlockSpec(memory_space=pltpu.VMEM)
    f32 = jnp.float32
    return pl.pallas_call(
        finish_kernel,
        out_shape=(
            jax.ShapeDtypeStruct((1, TILE, DOUT), f32),
            jax.ShapeDtypeStruct((DIN, DOUT), f32),
            jax.ShapeDtypeStruct((DIN, DOUT), f32),
            jax.ShapeDtypeStruct((1, DOUT), f32),
        ),
        in_specs=[vmem, pl.BlockSpec(memory_space=pl.ANY), vmem, vmem, vmem, vmem],
        out_specs=(vmem, vmem, vmem, vmem),
        scratch_shapes=[
            pltpu.VMEM((TILE, DIN), f32),
            pltpu.VMEM((3, 2 * TILE, DIN), f32),
            pltpu.VMEM((TILE, DIN), f32),
            pltpu.VMEM((TILE, DIN), f32),
            pltpu.VMEM((2, 264, 128), f32),
            pltpu.VMEM((264, 128), f32),
            pltpu.VMEM((2, NX, 72, 128), f32),
            pltpu.VMEM((2, NY, 16, 128), f32),
            pltpu.VMEM((1 + NZ, 16, 128), f32),
            pltpu.VMEM((2, 256, 128), f32),
            dma(()),
            dma((3,)),
            dma((3,)),
            dma(()),
            dma(()),
            dma((2,)),
            dma((2,)),
            dma((2, NX)),
            dma((2, NX)),
            dma((2, NY)),
            dma((2, NY)),
            dma((NZ,)),
            dma((NZ,)),
        ],
        compiler_params=pltpu.CompilerParams(
            collective_id=1, has_side_effects=True, vmem_limit_bytes=20 * 2**20
        ),
        name="finish",
    )(part, features, w_self, w_neigh, bias, cotangent)


def on_device(
    features, self_weight, neigh_weight, bias, edge_tiles, tile_rows, tile_cols, tile_count, cotangent
):
    got = spread(pltpu.with_memory_space_constraint(features, pltpu.HBM))
    part = products(tile_rows, tile_cols, tile_count, got, edge_tiles)
    out, gs, gn, gb = finish(part, features, self_weight, neigh_weight, bias.reshape(1, DOUT), cotangent)
    return out, gs, gn, gb.reshape(DOUT)


def solution(mesh):
    in_specs = (
        P("col", None, None),
        P(),
        P(),
        P(),
        P("row", "col", None, None, None),
        P("row", "col", None),
        P("row", "col", None),
        P("row", "col", None),
        P("col", "row", None),
    )
    out_specs = (P("col", "row", None), P(), P(), P())
    return jax.shard_map(on_device, mesh=mesh, in_specs=in_specs, out_specs=out_specs, check_vma=False)
```

```python
import jax
import jax.numpy as jnp
from jax import lax
from jax.experimental import pallas as pl
from jax.experimental.pallas import tpu as pltpu
from jax.sharding import PartitionSpec as P

MESH = pl.DeviceIdType.MESH
TILE = 128
KT = 8
G = 1024
DIN = 128
DOUT = 256
STOPS = 8
TS = 12
NX, NY, NZ = 4, 8, 8
PR = G // NX
NS = 4
PART = PR // NS
PACK = 8


class Place:
    def __init__(self):
        self.r = lax.axis_index("row")
        c = lax.axis_index("col")
        self.x = lax.div(self.r, 2)
        self.zh = lax.rem(self.r, 2)
        self.y = lax.div(c, 8)
        k = lax.rem(c, 8)
        self.zl = lax.div(k, 2)
        self.core = lax.rem(k, 2)
        self.z = self.zh * 4 + self.zl

    def dev(self, x=None, y=None, z=None, core=None):
        x = self.x if x is None else x
        y = self.y if y is None else y
        z = self.z if z is None else z
        core = self.core if core is None else core
        return (x * 2 + lax.div(z, 4), y * 8 + lax.rem(z, 4) * 2 + core)


def rows_of(ref, plane, p, rows=PR):
    return ref.at[plane, pl.ds(pl.multiple_of(p * rows, rows), rows)]


def remote(src, dst, send, recv, dev):
    return pltpu.make_async_remote_copy(
        src_ref=src, dst_ref=dst, send_sem=send, recv_sem=recv, device_id=dev, device_id_type=MESH
    )


def greet(devs):
    barrier = pltpu.get_barrier_semaphore()
    for dev in devs:
        pl.semaphore_signal(barrier, inc=1, device_id=dev, device_id_type=MESH)
    return barrier


def spread_kernel(
    feat,
    got,
    walk,
    walk2,
    b_buf,
    y_send,
    y_recv,
    w_send,
    w_recv,
    x_send,
    ab_recv,
    x2_send,
    seam_send,
    z_send,
    g_recv,
    s_send,
    s_recv,
    loc,
):
    me = Place()
    x, z, zl, zh, core = me.x, me.z, me.zl, me.zh, me.core
    y_at = {d: me.dev(y=lax.rem(me.y + d, NY)) for d in (1, 2, 6, 7)}
    z_at = {d: me.dev(z=lax.rem(z + d, NZ)) for d in (1, 2, 6, 7)}
    x_at = [me.dev(x=lax.rem(x + d, NX)) for d in range(NX)]
    other = me.dev(core=1 - core)
    low_seam = z == 3
    high_seam = z == 4
    seam = jnp.logical_or(low_seam, high_seam)
    far = jnp.where(low_seam, 4, 3)
    barrier = greet(list(y_at.values()) + list(z_at.values()) + x_at[1:] + [other])

    @pl.when(seam)
    def _():
        greet([me.dev(x=lax.rem(x + d, NX), z=far) for d in range(1, NX)])

    load = pltpu.make_async_copy(feat.at[0, pl.ds(pl.multiple_of(x * PR, PR), PR)], walk.at[0], loc)
    load.start()
    load.wait()
    pl.semaphore_wait(barrier, 12 + 3 * seam.astype(jnp.int32))

    def y_copy(src, dst, d):
        return remote(walk.at[src], walk.at[dst], y_send.at[dst], y_recv.at[dst, 0], y_at[d])

    def y_part(src, dst, d, s):
        at = pl.ds(s * PART, PART)
        return remote(walk.at[src, at], walk.at[dst, at], y_send.at[dst], y_recv.at[dst, s], y_at[d])

    half = PR // 2

    def piece(plane, p, j=None):
        ref = b_buf if plane == 1 else got.at[plane]
        if j is None:
            return ref.at[pl.ds(pl.multiple_of(p * PR, PR), PR)]
        return ref.at[pl.ds(pl.multiple_of(p * PR + j * half, half), half)]

    def walked(h, j):
        return walk.at[h] if j is None else walk.at[h, pl.ds(j * half, half)]

    def x_copy(h, v, j):
        to = h // 2 if v == 0 else lax.rem(h // 2 - zh + NX, NX)
        dev = me.dev(x=jnp.int32(to))
        return to, remote(walked(h, j), piece(v, x, j), x_send.at[h], ab_recv.at[v, x, j or 0], dev)

    def seam_copy(h, low, j):
        to = lax.rem(jnp.int32(h // 2 + (NX - 1 if low else 0)), NX)
        plane = 2 if low else 6
        side = 0 if low else 1
        dev = me.dev(x=to, z=jnp.int32(4 if low else 3))
        return remote(walked(h, j), piece(plane, x, j), seam_send.at[h], g_recv.at[side, x], dev)

    def across(h, j=None, finish=False):
        for v in (0, 1):
            fits = zh == h % 2 if v == 0 else zh != h % 2

            @pl.when(fits)
            def _():
                to, copy = x_copy(h, v, j)

                @pl.when(to != x)
                def _():
                    copy.wait_send() if finish else copy.start()

                if not finish:

                    @pl.when(to == x)
                    def _():
                        pltpu.make_async_copy(walked(h, j), piece(v, x, j), ab_recv.at[v, x, j]).start()

        if h % 2 == 0:
            for low, fits in ((True, low_seam), (False, high_seam)):

                @pl.when(fits)
                def _():
                    copy = seam_copy(h, low, j)
                    copy.wait_send() if finish else copy.start()

    def up_copy(p, j=None):
        return remote(piece(0, p, j), piece(2, p, j), z_send.at[0, p], g_recv.at[0, p], z_at[1])

    def down_copy(p, j=None):
        return remote(piece(1, p, j), piece(6, p, j), z_send.at[1, p], g_recv.at[1, p], z_at[7])

    def own_swap(v, p):
        return remote(piece(v, p), rows_of(got, 1, p), s_send.at[0], s_recv.at[0], other)

    def swap(n, p):
        return remote(rows_of(got, 2 * n, p), rows_of(got, 2 * n + 1, p), s_send.at[n], s_recv.at[n], other)

    def swapped(n):
        return remote(got.at[2 * n], got.at[2 * n + 1], s_send.at[n], s_recv.at[n], other)

    def pass_on(v):
        for j in range(2):
            for p in range(NX):
                remote(walked(0, j), piece(v, p, j), x_send.at[0], ab_recv.at[v, p, j], other).wait_recv()

                @pl.when(jnp.logical_not(low_seam if v == 0 else high_seam))
                def _():
                    (up_copy(p, j) if v == 0 else down_copy(p, j)).start()

                if j == 1:

                    @pl.when(core == v)
                    def _():
                        own_swap(v, p).start()

    near_a = jnp.minimum(me.r, 8 - me.r)
    next_r = lax.rem(me.r + 1, 8)
    near_b = jnp.minimum(next_r, 8 - next_r)

    def pass_near(n):
        for v, near in ((0, near_a), (1, near_b)):

            @pl.when(near == n)
            def _():
                pass_on(v)

    even = jnp.logical_xor(zl >= 2, zh == 1)
    two = jnp.where(core == 0, 2, 6)
    ahead = remote(walk.at[0], walk2.at[0], w_send.at[0], w_recv.at[0], me.dev(z=lax.rem(z + two, NZ)))
    def w_copy(src, dst, d):
        return remote(walk2.at[src], walk2.at[dst], w_send.at[dst], w_recv.at[dst], y_at[d])

    def w_half(src, dst, d, n):
        at = pl.ds(n * half, half)
        sem = dst if n == 0 else 8
        return remote(walk2.at[src, at], walk2.at[dst, at], w_send.at[sem], w_recv.at[sem], y_at[d])

    def across2(h, finish=False):
        to = jnp.where(zl >= 2, h // 2, lax.rem(h // 2 - zh + NX, NX))
        copy = remote(walk2.at[h], rows_of(got, 4, x), x2_send.at[h], g_recv.at[2, x], me.dev(x=to))

        @pl.when(to != x)
        def _():
            copy.wait_send() if finish else copy.start()

        if not finish:

            @pl.when(to == x)
            def _():
                pltpu.make_async_copy(walk2.at[h], rows_of(got, 4, x), g_recv.at[2, x]).start()

    def w_start():
        ahead.wait_recv()

        @pl.when(even)
        def _():
            w_copy(0, 2, 2).start()
            w_copy(0, 6, 6).start()
            across2(0)

        @pl.when(jnp.logical_not(even))
        def _():
            w_copy(0, 1, 1).start()
            w_copy(0, 7, 7).start()

    def w_near():
        @pl.when(even)
        def _():
            w_copy(2, 2, 2).wait_recv()
            w_half(2, 4, 2, 0).start()
            w_copy(6, 6, 6).wait_recv()
            w_half(6, 4, 6, 1).start()
            across2(2)
            across2(6)

        @pl.when(jnp.logical_not(even))
        def _():
            w_copy(1, 1, 1).wait_recv()
            w_copy(1, 3, 2).start()
            w_copy(7, 7, 7).wait_recv()
            w_copy(7, 5, 6).start()
            across2(1)
            across2(7)

    def w_far():
        @pl.when(even)
        def _():
            w_half(2, 4, 2, 0).wait_recv()
            w_half(6, 4, 6, 1).wait_recv()
            across2(4)

        @pl.when(jnp.logical_not(even))
        def _():
            w_copy(3, 3, 2).wait_recv()
            across2(3)
            w_copy(5, 5, 6).wait_recv()
            across2(5)

    for s in range(NS):
        y_part(0, 1, 1, s).start()
        y_part(0, 7, 7, s).start()
    ahead.start()
    across(0, 0)
    across(0, 1)
    for n in range(1, 5):
        for s in range(NS):
            first = s < NS // 2
            if n < 4 or first:
                y_part(n, n, 1, s).wait_recv()
            if n < 3 or (n == 3 and first):
                y_part(n, n + 1, 1, s).start()
            if n < 4 or not first:
                y_part(8 - n, 8 - n, 7, s).wait_recv()
            if n < 3 or (n == 3 and not first):
                y_part(8 - n, 7 - n, 7, s).start()
            if s % (NS // 2) == NS // 2 - 1 and n < 4:
                across(n, s // (NS // 2))
                across(8 - n, s // (NS // 2))
        if n == 4:
            across(4, 0)
            across(4, 1)
        if n == 3:
            w_start()
        if n >= 2:
            pass_near(n - 2)
    w_near()
    pass_near(3)
    pass_near(4)
    w_far()

    for p in range(NX):
        up_copy(p).wait_recv()
        swap(1, p).start()
        down_copy(p).wait_recv()
        swap(3, p).start()
    for p in range(NX):
        remote(walk.at[0], rows_of(got, 4, p), x2_send.at[0], g_recv.at[2, p], other).wait_recv()
        swap(2, p).start()

    for n in (0, 1, 3, 2):
        swapped(n).wait_recv()
        swapped(n).wait_send()
    for p in range(NX):

        @pl.when(jnp.logical_not(low_seam))
        def _():
            up_copy(p).wait_send()

        @pl.when(jnp.logical_not(high_seam))
        def _():
            down_copy(p).wait_send()

    for h in range(8):
        across(h, finish=True)
        if h:
            y_copy(h, h, 1).wait_send()
    ahead.wait_send()

    @pl.when(even)
    def _():
        for h in (0, 2, 4, 6):
            across2(h, finish=True)
        w_copy(2, 2, 2).wait_send()
        w_copy(6, 6, 6).wait_send()
        w_half(2, 4, 2, 0).wait_send()
        w_half(6, 4, 6, 1).wait_send()

    @pl.when(jnp.logical_not(even))
    def _():
        for h in (1, 3, 5, 7):
            across2(h, finish=True)
            w_copy(h, h, 1).wait_send()


def spread(features):
    dma = pltpu.SemaphoreType.DMA
    return pl.pallas_call(
        spread_kernel,
        out_shape=jax.ShapeDtypeStruct((8, G, DIN), jnp.float32),
        in_specs=[pl.BlockSpec(memory_space=pltpu.HBM)],
        out_specs=pl.BlockSpec(memory_space=pltpu.VMEM),
        scratch_shapes=[
            pltpu.VMEM((8, PR, DIN), jnp.float32),
            pltpu.VMEM((8, PR, DIN), jnp.float32),
            pltpu.VMEM((G, DIN), jnp.float32),
            dma((8,)),
            dma((8, NS)),
            dma((9,)),
            dma((9,)),
            dma((8,)),
            dma((2, NX, 2)),
            dma((8,)),
            dma((8,)),
            dma((2, NX)),
            dma((3, NX)),
            dma((4,)),
            dma((4,)),
            dma(()),
        ],
        compiler_params=pltpu.CompilerParams(
            collective_id=0, has_side_effects=True, vmem_limit_bytes=20 * 2**20
        ),
        name="spread",
    )(features)


def products_kernel(rows, cols, counts, got, tiles, part):
    core = lax.rem(lax.axis_index("col"), 2)
    part[...] = jnp.zeros_like(part)

    def stop(s, carry):
        plane = jnp.where(jnp.logical_and(core == 0, lax.rem(s, 2) == 1), lax.rem(s + 2, 8), s)
        count = counts[0, 0, s]
        prods = []
        for t in range(TS):
            q = s * TS + t
            col = pl.multiple_of(cols[0, 0, q] * TILE, TILE)
            chosen = got[plane, pl.ds(col, TILE), :]
            chosen = jnp.where(t < count, chosen, 0.0)
            high = chosen.astype(jnp.bfloat16)
            low = (chosen - high.astype(jnp.float32)).astype(jnp.bfloat16)
            both = jnp.dot(
                tiles[0, 0, q], jnp.concatenate([high, low], axis=1), preferred_element_type=jnp.float32
            )
            prods.append(both[:, :DIN] + both[:, DIN:])
        for t in range(TS):
            at = pl.ds(pl.multiple_of(rows[0, 0, s * TS + t] * TILE, TILE), TILE)
            part[at, :] = part[at, :] + prods[t]
        return carry

    lax.fori_loop(0, STOPS, stop, 0)


def products(rows, cols, counts, got, tiles):
    smem = pl.BlockSpec(memory_space=pltpu.SMEM)
    vmem = pl.BlockSpec(memory_space=pltpu.VMEM)
    return pl.pallas_call(
        products_kernel,
        out_shape=jax.ShapeDtypeStruct((G, DIN), jnp.float32),
        in_specs=[smem, smem, smem, vmem, vmem],
        out_specs=vmem,
        compiler_params=pltpu.CompilerParams(vmem_limit_bytes=20 * 2**20),
        name="products",
    )(rows, cols, counts, got, tiles)


def exact(a, b, dims=((1,), (0,))):
    return lax.dot_general(
        a, b, (dims, ((), ())), precision=lax.Precision.HIGHEST, preferred_element_type=jnp.float32
    )


def finish_kernel(
    part,
    feat,
    w_self,
    w_neigh,
    bias,
    cot,
    out,
    mine,
    g_bias,
    own,
    rs_in,
    half_in,
    half_out,
    packs,
    pack_in,
    xs,
    ys,
    zs,
    loc,
    rs_send,
    rs_recv,
    h_send,
    h_recv,
    c_send,
    c_recv,
    x_send,
    x_recv,
    y_send,
    y_recv,
    z_send,
    z_recv,
):
    me = Place()
    r, x, y, z, core = me.r, me.x, me.y, me.z, me.core
    x_dev = [me.dev(x=lax.rem(x + d, NX)) for d in range(NX)]
    y_dev = [me.dev(y=lax.rem(y + d, NY)) for d in range(NY)]
    z_dev = [me.dev(z=lax.rem(z + d, NZ)) for d in range(NZ)]
    other = me.dev(core=1 - core)
    barrier = greet(x_dev[1:] + y_dev[1:] + z_dev[1:] + [other])
    load = pltpu.make_async_copy(feat.at[0, pl.ds(pl.multiple_of(r * TILE, TILE), TILE)], own, loc)
    load.start()
    pl.semaphore_wait(barrier, NX + NY + NZ - 2)

    hr = TILE // 2

    def to_x(d, n):
        there = 2 * lax.rem(x + d, NX)
        if n < 2:
            src = part.at[pl.ds(pl.multiple_of((there + 1 - me.zh) * TILE + n * hr, hr), hr)]
            dst = rs_in.at[d - 1, pl.ds(n * hr, hr)]
        else:
            src = part.at[pl.ds(pl.multiple_of((there + me.zh) * TILE, TILE), TILE)]
            dst = rs_in.at[d - 1, pl.ds(TILE, TILE)]
        return remote(src, dst, rs_send.at[d - 1, n], rs_recv.at[d - 1, n], x_dev[d])

    def over(n):
        at = pl.ds(n * hr, hr)
        return remote(half_out.at[at], half_in.at[at], h_send.at[n], h_recv.at[n], z_dev[4])

    for n in range(3):
        for d in (2, 1, 3):
            to_x(d, n).start()
    for n in range(2):
        for d in (1, 3, 2):
            to_x(d, n).wait_recv()
        at = pl.ds(n * hr, hr)
        away = pl.ds(pl.multiple_of((2 * x + 1 - me.zh) * TILE + n * hr, hr), hr)
        half_out[at, :] = part[away, :] + rs_in[0, at, :] + rs_in[1, at, :] + rs_in[2, at, :]
        over(n).start()
    for d in (1, 3, 2):
        to_x(d, 2).wait_recv()
    at = pl.ds(TILE, TILE)
    home = pl.ds(pl.multiple_of((2 * x + me.zh) * TILE, TILE), TILE)
    kept = part[home, :] + rs_in[0, at, :] + rs_in[1, at, :] + rs_in[2, at, :]
    load.wait()
    mine_rows = own[...]
    start = exact(mine_rows, w_self[...]) + bias[...]
    over(0).wait_recv()
    over(1).wait_recv()
    agg = kept + half_in[...]

    v = start + exact(agg, w_neigh[...])
    a = 0.7978845608028654
    b = 0.044715
    t = jnp.tanh(a * (v + b * (v * v * v)))
    hidden = 0.5 * v * (1.0 + t)
    scale = lax.rsqrt(jnp.mean(hidden * hidden, axis=-1, keepdims=True) + 1e-06)
    out[0] = hidden * scale
    g = cot[0]
    dot = jnp.mean(g * hidden, axis=-1, keepdims=True)
    d_hidden = scale * (g - hidden * (scale * scale * dot))
    slope = 0.5 * (1.0 + t) + 0.5 * v * (1.0 - t * t) * (a * (1.0 + 3.0 * b * (v * v)))
    d_pre = d_hidden * slope
    gs = exact(mine_rows, d_pre, ((0,), (0,)))
    gn = exact(agg, d_pre, ((0,), (0,)))
    gb = jnp.sum(d_pre, axis=0, keepdims=True)

    packs[0, 0:128, :] = gs[:, :128]
    packs[0, 128:256, :] = gs[:, 128:]
    packs[1, 0:128, :] = gn[:, :128]
    packs[1, 128:256, :] = gn[:, 128:]
    first = jnp.broadcast_to(gb[:, :128], (PACK, 128))
    second = jnp.broadcast_to(gb[:, 128:], (PACK, 128))
    gbp = jnp.where(lax.broadcasted_iota(jnp.int32, (PACK, 128), 0) == 0, first, second)
    packs[0, 256:264, :] = gbp
    packs[1, 256:264, :] = gbp
    core_swap = remote(packs.at[1 - core], pack_in, c_send.at[0], c_recv.at[0], other)
    core_swap.start()
    core_swap.wait_recv()
    b_now = gbp + pack_in[256:264, :]

    def piece(n, size):
        at = pl.ds(pl.multiple_of(n * size, size), size)
        return packs[core, at, :] + pack_in[at, :]

    for n in range(NX):
        xs[0, n, 0:64, :] = piece(n, 64)
        xs[0, n, 64:72, :] = b_now

    def x_copy(d):
        return remote(
            xs.at[0, lax.rem(x + d, NX)], xs.at[1, x], x_send.at[0, d], x_recv.at[0, x], x_dev[d]
        )

    def x_wait(d):
        src = lax.rem(x + NX - d, NX)
        remote(xs.at[0, 0], xs.at[1, src], x_send.at[0, d], x_recv.at[0, src], x_dev[d]).wait_recv()

    for d in (2, 1, 3):
        x_copy(d).start()
    xs[1, x] = xs[0, x]
    for d in (1, 3, 2):
        x_wait(d)
    x_sum = xs[1, 0] + xs[1, 1] + xs[1, 2] + xs[1, 3]

    for n in range(NY):
        ys[0, n, 0:8, :] = x_sum[n * 8 : n * 8 + 8]
        ys[0, n, 8:16, :] = x_sum[64:72]

    def y_copy(d):
        return remote(
            ys.at[0, lax.rem(y + d, NY)], ys.at[1, y], y_send.at[0, d], y_recv.at[0, y], y_dev[d]
        )

    def y_wait(d):
        src = lax.rem(y + NY - d, NY)
        remote(ys.at[0, 0], ys.at[1, src], y_send.at[0, d], y_recv.at[0, src], y_dev[d]).wait_recv()

    order = (4, 3, 5, 2, 6, 1, 7)
    for d in order:
        y_copy(d).start()
    ys[1, y] = ys[0, y]
    for d in order[::-1]:
        y_wait(d)
    y_sum = ys[1, 0]
    for n in range(1, NY):
        y_sum = y_sum + ys[1, n]

    zs[0] = y_sum
    zs[1 + z] = y_sum

    def z_copy(d):
        return remote(zs.at[0], zs.at[1 + z], z_send.at[d], z_recv.at[z], z_dev[d])

    def z_wait(d):
        src = lax.rem(z + NZ - d, NZ)
        remote(zs.at[0], zs.at[1 + src], z_send.at[d], z_recv.at[src], z_dev[d]).wait_recv()

    for d in order:
        z_copy(d).start()
    for d in order[::-1]:
        z_wait(d)
    z_sum = zs[1]
    for n in range(1, NZ):
        z_sum = z_sum + zs[1 + n]
    g_bias[:, 0:128] = z_sum[8:9]
    g_bias[:, 128:256] = z_sum[9:10]

    def at_y(n):
        return mine.at[core, pl.ds(pl.multiple_of(x * 64 + n * 8, 8), 8)]

    def y_back(d):
        return remote(at_y(y), at_y(y), y_send.at[1, d], y_recv.at[1, y], y_dev[d])

    def y_back_wait(d):
        src = lax.rem(y + NY - d, NY)
        remote(at_y(src), at_y(src), y_send.at[1, d], y_recv.at[1, src], y_dev[d]).wait_recv()

    mine[core, pl.ds(pl.multiple_of(x * 64 + y * 8, 8), 8), :] = z_sum[0:8]
    for d in order:
        y_back(d).start()
    for d in order[::-1]:
        y_back_wait(d)

    def at_x(n):
        return mine.at[core, pl.ds(pl.multiple_of(n * 64, 64), 64)]

    def x_back(d):
        return remote(at_x(x), at_x(x), x_send.at[1, d], x_recv.at[1, x], x_dev[d])

    def x_back_wait(d):
        src = lax.rem(x + NX - d, NX)
        remote(at_x(src), at_x(src), x_send.at[1, d], x_recv.at[1, src], x_dev[d]).wait_recv()

    for d in (2, 1, 3):
        x_back(d).start()
    for d in (1, 3, 2):
        x_back_wait(d)
    core_back = remote(mine.at[core], mine.at[core], c_send.at[1], c_recv.at[1], other)
    core_back_in = remote(mine.at[1 - core], mine.at[1 - core], c_send.at[1], c_recv.at[1], other)
    core_back.start()
    core_back_in.wait_recv()

    for d in (1, 2, 3):
        for n in range(3):
            to_x(d, n).wait_send()
        x_copy(d).wait_send()
        x_back(d).wait_send()
    over(0).wait_send()
    over(1).wait_send()
    core_swap.wait_send()
    core_back.wait_send()
    for d in range(1, 8):
        y_copy(d).wait_send()
        z_copy(d).wait_send()
        y_back(d).wait_send()


def finish(part, features, w_self, w_neigh, bias, cotangent):
    dma = pltpu.SemaphoreType.DMA
    vmem = pl.BlockSpec(memory_space=pltpu.VMEM)
    f32 = jnp.float32
    return pl.pallas_call(
        finish_kernel,
        out_shape=(
            jax.ShapeDtypeStruct((1, TILE, DOUT), f32),
            jax.ShapeDtypeStruct((2, 2 * DIN, 128), f32),
            jax.ShapeDtypeStruct((1, DOUT), f32),
        ),
        in_specs=[vmem, pl.BlockSpec(memory_space=pl.ANY), vmem, vmem, vmem, vmem],
        out_specs=(vmem, vmem, vmem),
        scratch_shapes=[
            pltpu.VMEM((TILE, DIN), f32),
            pltpu.VMEM((3, 2 * TILE, DIN), f32),
            pltpu.VMEM((TILE, DIN), f32),
            pltpu.VMEM((TILE, DIN), f32),
            pltpu.VMEM((2, 264, 128), f32),
            pltpu.VMEM((264, 128), f32),
            pltpu.VMEM((2, NX, 72, 128), f32),
            pltpu.VMEM((2, NY, 16, 128), f32),
            pltpu.VMEM((1 + NZ, 16, 128), f32),
            dma(()),
            dma((3, 3)),
            dma((3, 3)),
            dma((2,)),
            dma((2,)),
            dma((2,)),
            dma((2,)),
            dma((2, NX)),
            dma((2, NX)),
            dma((2, NY)),
            dma((2, NY)),
            dma((NZ,)),
            dma((NZ,)),
        ],
        compiler_params=pltpu.CompilerParams(
            collective_id=1, has_side_effects=True, vmem_limit_bytes=20 * 2**20
        ),
        name="finish",
    )(part, features, w_self, w_neigh, bias, cotangent)


def emit_kernel(o, m, b, out, g_self, g_neigh, g_bias, sems):
    moves = [(o, out), (b, g_bias)]
    for n, g in enumerate((g_self, g_neigh)):
        for h in range(2):
            moves.append((m.at[n, pl.ds(h * DIN, DIN)], g.at[:, pl.ds(h * 128, 128)]))
    copies = [pltpu.make_async_copy(src, dst, sems.at[i]) for i, (src, dst) in enumerate(moves)]
    for copy in copies:
        copy.start()
    for copy in copies:
        copy.wait()


def emit(out, grads, g_bias):
    f32 = jnp.float32
    vmem = pl.BlockSpec(memory_space=pltpu.VMEM)
    hbm = pl.BlockSpec(memory_space=pltpu.HBM)
    return pl.pallas_call(
        emit_kernel,
        out_shape=(
            jax.ShapeDtypeStruct((1, TILE, DOUT), f32),
            jax.ShapeDtypeStruct((DIN, DOUT), f32),
            jax.ShapeDtypeStruct((DIN, DOUT), f32),
            jax.ShapeDtypeStruct((1, DOUT), f32),
        ),
        in_specs=[vmem, vmem, vmem],
        out_specs=(hbm, hbm, hbm, hbm),
        scratch_shapes=[pltpu.SemaphoreType.DMA((6,))],
        compiler_params=pltpu.CompilerParams(vmem_limit_bytes=4 * 2**20),
        name="emit",
    )(out, grads, g_bias)


def on_device(
    features, self_weight, neigh_weight, bias, edge_tiles, tile_rows, tile_cols, tile_count, cotangent
):
    got = spread(pltpu.with_memory_space_constraint(features, pltpu.HBM))
    part = products(tile_rows, tile_cols, tile_count, got, edge_tiles)
    done = finish(part, features, self_weight, neigh_weight, bias.reshape(1, DOUT), cotangent)
    out, gs, gn, gb = emit(*done)
    return out, gs, gn, gb.reshape(DOUT)


def solution(mesh):
    in_specs = (
        P("col", None, None),
        P(),
        P(),
        P(),
        P("row", "col", None, None, None),
        P("row", "col", None),
        P("row", "col", None),
        P("row", "col", None),
        P("col", "row", None),
    )
    out_specs = (P("col", "row", None), P(), P(), P())
    return jax.shard_map(on_device, mesh=mesh, in_specs=in_specs, out_specs=out_specs, check_vma=False)
```

```python
import jax
import jax.numpy as jnp
from jax import lax
from jax.experimental import pallas as pl
from jax.experimental.pallas import tpu as pltpu
from jax.sharding import PartitionSpec as P

MESH = pl.DeviceIdType.MESH
TILE = 128
KT = 8
G = 1024
DIN = 128
DOUT = 256
STOPS = 8
TS = 12
NX, NY, NZ = 4, 8, 8
PR = G // NX
NS = 4
PART = PR // NS
PACK = 8


class Place:
    def __init__(self):
        self.r = lax.axis_index("row")
        c = lax.axis_index("col")
        self.x = lax.div(self.r, 2)
        self.zh = lax.rem(self.r, 2)
        self.y = lax.div(c, 8)
        k = lax.rem(c, 8)
        self.zl = lax.div(k, 2)
        self.core = lax.rem(k, 2)
        self.z = self.zh * 4 + self.zl

    def dev(self, x=None, y=None, z=None, core=None):
        x = self.x if x is None else x
        y = self.y if y is None else y
        z = self.z if z is None else z
        core = self.core if core is None else core
        return (x * 2 + lax.div(z, 4), y * 8 + lax.rem(z, 4) * 2 + core)


def rows_of(ref, plane, p, rows=PR):
    return ref.at[plane, pl.ds(pl.multiple_of(p * rows, rows), rows)]


def remote(src, dst, send, recv, dev):
    return pltpu.make_async_remote_copy(
        src_ref=src, dst_ref=dst, send_sem=send, recv_sem=recv, device_id=dev, device_id_type=MESH
    )


def greet(devs):
    barrier = pltpu.get_barrier_semaphore()
    for dev in devs:
        pl.semaphore_signal(barrier, inc=1, device_id=dev, device_id_type=MESH)
    return barrier


def spread_kernel(
    feat,
    got,
    walk,
    walk2,
    b_buf,
    y_send,
    y_recv,
    w_send,
    w_recv,
    x_send,
    ab_recv,
    x2_send,
    seam_send,
    z_send,
    g_recv,
    s_send,
    s_recv,
    loc,
):
    me = Place()
    x, z, zl, zh, core = me.x, me.z, me.zl, me.zh, me.core
    y_at = {d: me.dev(y=lax.rem(me.y + d, NY)) for d in (1, 2, 6, 7)}
    z_at = {d: me.dev(z=lax.rem(z + d, NZ)) for d in (1, 2, 6, 7)}
    x_at = [me.dev(x=lax.rem(x + d, NX)) for d in range(NX)]
    other = me.dev(core=1 - core)
    low_seam = z == 3
    high_seam = z == 4
    seam = jnp.logical_or(low_seam, high_seam)
    far = jnp.where(low_seam, 4, 3)
    barrier = greet(list(y_at.values()) + list(z_at.values()) + x_at[1:] + [other])

    @pl.when(seam)
    def _():
        greet([me.dev(x=lax.rem(x + d, NX), z=far) for d in range(1, NX)])

    load = pltpu.make_async_copy(feat.at[0, pl.ds(pl.multiple_of(x * PR, PR), PR)], walk.at[0], loc)
    load.start()
    load.wait()
    pl.semaphore_wait(barrier, 12 + 3 * seam.astype(jnp.int32))

    def y_copy(src, dst, d):
        return remote(walk.at[src], walk.at[dst], y_send.at[dst], y_recv.at[dst, 0], y_at[d])

    def y_part(src, dst, d, s):
        at = pl.ds(s * PART, PART)
        return remote(walk.at[src, at], walk.at[dst, at], y_send.at[dst], y_recv.at[dst, s], y_at[d])

    half = PR // 2

    def piece(plane, p, j=None):
        ref = b_buf if plane == 1 else got.at[plane]
        if j is None:
            return ref.at[pl.ds(pl.multiple_of(p * PR, PR), PR)]
        return ref.at[pl.ds(pl.multiple_of(p * PR + j * half, half), half)]

    def walked(h, j):
        return walk.at[h] if j is None else walk.at[h, pl.ds(j * half, half)]

    def x_copy(h, v, j):
        to = h // 2 if v == 0 else lax.rem(h // 2 - zh + NX, NX)
        dev = me.dev(x=jnp.int32(to))
        return to, remote(walked(h, j), piece(v, x, j), x_send.at[h], ab_recv.at[v, x, j or 0], dev)

    def seam_copy(h, low, j):
        to = lax.rem(jnp.int32(h // 2 + (NX - 1 if low else 0)), NX)
        plane = 2 if low else 6
        side = 0 if low else 1
        dev = me.dev(x=to, z=jnp.int32(4 if low else 3))
        return remote(walked(h, j), piece(plane, x, j), seam_send.at[h], g_recv.at[side, x], dev)

    def across(h, j=None, finish=False):
        for v in (0, 1):
            fits = zh == h % 2 if v == 0 else zh != h % 2

            @pl.when(fits)
            def _():
                to, copy = x_copy(h, v, j)

                @pl.when(to != x)
                def _():
                    copy.wait_send() if finish else copy.start()

                if not finish:

                    @pl.when(to == x)
                    def _():
                        pltpu.make_async_copy(walked(h, j), piece(v, x, j), ab_recv.at[v, x, j]).start()

        if h % 2 == 0:
            for low, fits in ((True, low_seam), (False, high_seam)):

                @pl.when(fits)
                def _():
                    copy = seam_copy(h, low, j)
                    copy.wait_send() if finish else copy.start()

    def up_copy(p, j=None):
        return remote(piece(0, p, j), piece(2, p, j), z_send.at[0, p], g_recv.at[0, p], z_at[1])

    def down_copy(p, j=None):
        return remote(piece(1, p, j), piece(6, p, j), z_send.at[1, p], g_recv.at[1, p], z_at[7])

    def own_swap(v, p):
        return remote(piece(v, p), rows_of(got, 1, p), s_send.at[0], s_recv.at[0], other)

    def swap(n, p):
        return remote(rows_of(got, 2 * n, p), rows_of(got, 2 * n + 1, p), s_send.at[n], s_recv.at[n], other)

    def swapped(n):
        return remote(got.at[2 * n], got.at[2 * n + 1], s_send.at[n], s_recv.at[n], other)

    def pass_on(v):
        for j in range(2):
            for p in range(NX):
                remote(walked(0, j), piece(v, p, j), x_send.at[0], ab_recv.at[v, p, j], other).wait_recv()

                @pl.when(jnp.logical_not(low_seam if v == 0 else high_seam))
                def _():
                    (up_copy(p, j) if v == 0 else down_copy(p, j)).start()

                if j == 1:

                    @pl.when(core == v)
                    def _():
                        own_swap(v, p).start()

    near_a = jnp.minimum(me.r, 8 - me.r)
    next_r = lax.rem(me.r + 1, 8)
    near_b = jnp.minimum(next_r, 8 - next_r)

    def pass_near(n):
        for v, near in ((0, near_a), (1, near_b)):

            @pl.when(near == n)
            def _():
                pass_on(v)

    even = jnp.logical_xor(zl >= 2, zh == 1)
    two = jnp.where(core == 0, 2, 6)
    ahead = remote(walk.at[0], walk2.at[0], w_send.at[0], w_recv.at[0], me.dev(z=lax.rem(z + two, NZ)))
    def w_copy(src, dst, d):
        return remote(walk2.at[src], walk2.at[dst], w_send.at[dst], w_recv.at[dst], y_at[d])

    def w_half(src, dst, d, n):
        at = pl.ds(n * half, half)
        sem = dst if n == 0 else 8
        return remote(walk2.at[src, at], walk2.at[dst, at], w_send.at[sem], w_recv.at[sem], y_at[d])

    def across2(h, finish=False):
        to = jnp.where(zl >= 2, h // 2, lax.rem(h // 2 - zh + NX, NX))
        copy = remote(walk2.at[h], rows_of(got, 4, x), x2_send.at[h], g_recv.at[2, x], me.dev(x=to))

        @pl.when(to != x)
        def _():
            copy.wait_send() if finish else copy.start()

        if not finish:

            @pl.when(to == x)
            def _():
                pltpu.make_async_copy(walk2.at[h], rows_of(got, 4, x), g_recv.at[2, x]).start()

    def w_start():
        ahead.wait_recv()

        @pl.when(even)
        def _():
            w_copy(0, 2, 2).start()
            w_copy(0, 6, 6).start()
            across2(0)

        @pl.when(jnp.logical_not(even))
        def _():
            w_copy(0, 1, 1).start()
            w_copy(0, 7, 7).start()

    def w_near():
        @pl.when(even)
        def _():
            w_copy(2, 2, 2).wait_recv()
            w_half(2, 4, 2, 0).start()
            w_copy(6, 6, 6).wait_recv()
            w_half(6, 4, 6, 1).start()
            across2(2)
            across2(6)

        @pl.when(jnp.logical_not(even))
        def _():
            w_copy(1, 1, 1).wait_recv()
            w_copy(1, 3, 2).start()
            w_copy(7, 7, 7).wait_recv()
            w_copy(7, 5, 6).start()
            across2(1)
            across2(7)

    def w_far():
        @pl.when(even)
        def _():
            w_half(2, 4, 2, 0).wait_recv()
            w_half(6, 4, 6, 1).wait_recv()
            across2(4)

        @pl.when(jnp.logical_not(even))
        def _():
            w_copy(3, 3, 2).wait_recv()
            across2(3)
            w_copy(5, 5, 6).wait_recv()
            across2(5)

    for s in range(NS):
        y_part(0, 1, 1, s).start()
        y_part(0, 7, 7, s).start()
    ahead.start()
    across(0, 0)
    across(0, 1)
    for n in range(1, 5):
        for s in range(NS):
            first = s < NS // 2
            if n < 4 or first:
                y_part(n, n, 1, s).wait_recv()
            if n < 3 or (n == 3 and first):
                y_part(n, n + 1, 1, s).start()
            if n < 4 or not first:
                y_part(8 - n, 8 - n, 7, s).wait_recv()
            if n < 3 or (n == 3 and not first):
                y_part(8 - n, 7 - n, 7, s).start()
            if s % (NS // 2) == NS // 2 - 1 and n < 4:
                across(n, s // (NS // 2))
                across(8 - n, s // (NS // 2))
        if n == 4:
            across(4, 0)
            across(4, 1)
        if n == 3:
            w_start()
        if n >= 2:
            pass_near(n - 2)
    w_near()
    pass_near(3)
    pass_near(4)
    w_far()

    for p in range(NX):
        up_copy(p).wait_recv()
        swap(1, p).start()
        down_copy(p).wait_recv()
        swap(3, p).start()
    for p in range(NX):
        remote(walk.at[0], rows_of(got, 4, p), x2_send.at[0], g_recv.at[2, p], other).wait_recv()
        swap(2, p).start()

    for n in (0, 1, 3, 2):
        swapped(n).wait_recv()
        swapped(n).wait_send()
    for p in range(NX):

        @pl.when(jnp.logical_not(low_seam))
        def _():
            up_copy(p).wait_send()

        @pl.when(jnp.logical_not(high_seam))
        def _():
            down_copy(p).wait_send()

    for h in range(8):
        across(h, finish=True)
        if h:
            y_copy(h, h, 1).wait_send()
    ahead.wait_send()

    @pl.when(even)
    def _():
        for h in (0, 2, 4, 6):
            across2(h, finish=True)
        w_copy(2, 2, 2).wait_send()
        w_copy(6, 6, 6).wait_send()
        w_half(2, 4, 2, 0).wait_send()
        w_half(6, 4, 6, 1).wait_send()

    @pl.when(jnp.logical_not(even))
    def _():
        for h in (1, 3, 5, 7):
            across2(h, finish=True)
            w_copy(h, h, 1).wait_send()


def spread(features):
    dma = pltpu.SemaphoreType.DMA
    return pl.pallas_call(
        spread_kernel,
        out_shape=jax.ShapeDtypeStruct((8, G, DIN), jnp.float32),
        in_specs=[pl.BlockSpec(memory_space=pltpu.HBM)],
        out_specs=pl.BlockSpec(memory_space=pltpu.VMEM),
        scratch_shapes=[
            pltpu.VMEM((8, PR, DIN), jnp.float32),
            pltpu.VMEM((8, PR, DIN), jnp.float32),
            pltpu.VMEM((G, DIN), jnp.float32),
            dma((8,)),
            dma((8, NS)),
            dma((9,)),
            dma((9,)),
            dma((8,)),
            dma((2, NX, 2)),
            dma((8,)),
            dma((8,)),
            dma((2, NX)),
            dma((3, NX)),
            dma((4,)),
            dma((4,)),
            dma(()),
        ],
        compiler_params=pltpu.CompilerParams(
            collective_id=0, has_side_effects=True, vmem_limit_bytes=20 * 2**20
        ),
        name="spread",
    )(features)


def products_kernel(rows, cols, counts, got, tiles, part):
    core = lax.rem(lax.axis_index("col"), 2)
    part[...] = jnp.zeros_like(part)

    def stop(s, carry):
        plane = jnp.where(jnp.logical_and(core == 0, lax.rem(s, 2) == 1), lax.rem(s + 2, 8), s)
        count = counts[0, 0, s]
        prods = []
        for t in range(TS):
            q = s * TS + t
            col = pl.multiple_of(cols[0, 0, q] * TILE, TILE)
            chosen = got[plane, pl.ds(col, TILE), :]
            chosen = jnp.where(t < count, chosen, 0.0)
            high = chosen.astype(jnp.bfloat16)
            low = (chosen - high.astype(jnp.float32)).astype(jnp.bfloat16)
            both = jnp.dot(
                tiles[0, 0, q], jnp.concatenate([high, low], axis=1), preferred_element_type=jnp.float32
            )
            prods.append(both[:, :DIN] + both[:, DIN:])
        for t in range(TS):
            at = pl.ds(pl.multiple_of(rows[0, 0, s * TS + t] * TILE, TILE), TILE)
            part[at, :] = part[at, :] + prods[t]
        return carry

    lax.fori_loop(0, STOPS, stop, 0)


def products(rows, cols, counts, got, tiles):
    smem = pl.BlockSpec(memory_space=pltpu.SMEM)
    vmem = pl.BlockSpec(memory_space=pltpu.VMEM)
    return pl.pallas_call(
        products_kernel,
        out_shape=jax.ShapeDtypeStruct((G, DIN), jnp.float32),
        in_specs=[smem, smem, smem, vmem, vmem],
        out_specs=vmem,
        compiler_params=pltpu.CompilerParams(vmem_limit_bytes=20 * 2**20),
        name="products",
    )(rows, cols, counts, got, tiles)


def split(a):
    high = a.astype(jnp.bfloat16)
    return high, (a - high.astype(jnp.float32)).astype(jnp.bfloat16)


def exact(a, b, dims=((1,), (0,))):
    def dot(p, q):
        return lax.dot_general(p, q, (dims, ((), ())), preferred_element_type=jnp.float32)

    a_high, a_low = split(a)
    b_high, b_low = split(b)
    return dot(a_high, b_high) + (dot(a_high, b_low) + dot(a_low, b_high))


def finish_kernel(
    part,
    feat,
    w_self,
    w_neigh,
    bias,
    cot,
    out,
    mine,
    g_bias,
    own,
    rs_in,
    half_in,
    half_out,
    packs,
    pack_in,
    xs,
    ys,
    zs,
    loc,
    rs_send,
    rs_recv,
    h_send,
    h_recv,
    c_send,
    c_recv,
    x_send,
    x_recv,
    y_send,
    y_recv,
    z_send,
    z_recv,
):
    me = Place()
    r, x, y, z, core = me.r, me.x, me.y, me.z, me.core
    x_dev = [me.dev(x=lax.rem(x + d, NX)) for d in range(NX)]
    y_dev = [me.dev(y=lax.rem(y + d, NY)) for d in range(NY)]
    z_dev = [me.dev(z=lax.rem(z + d, NZ)) for d in range(NZ)]
    other = me.dev(core=1 - core)
    barrier = greet(x_dev[1:] + y_dev[1:] + z_dev[1:] + [other])
    load = pltpu.make_async_copy(feat.at[0, pl.ds(pl.multiple_of(r * TILE, TILE), TILE)], own, loc)
    load.start()
    pl.semaphore_wait(barrier, NX + NY + NZ - 2)

    hr = TILE // 2

    def to_x(d, n):
        there = 2 * lax.rem(x + d, NX)
        if n < 2:
            src = part.at[pl.ds(pl.multiple_of((there + 1 - me.zh) * TILE + n * hr, hr), hr)]
            dst = rs_in.at[d - 1, pl.ds(n * hr, hr)]
        else:
            src = part.at[pl.ds(pl.multiple_of((there + me.zh) * TILE, TILE), TILE)]
            dst = rs_in.at[d - 1, pl.ds(TILE, TILE)]
        return remote(src, dst, rs_send.at[d - 1, n], rs_recv.at[d - 1, n], x_dev[d])

    def over(n):
        at = pl.ds(n * hr, hr)
        return remote(half_out.at[at], half_in.at[at], h_send.at[n], h_recv.at[n], z_dev[4])

    for n in range(3):
        for d in (2, 1, 3):
            to_x(d, n).start()
    for n in range(2):
        for d in (1, 3, 2):
            to_x(d, n).wait_recv()
        at = pl.ds(n * hr, hr)
        away = pl.ds(pl.multiple_of((2 * x + 1 - me.zh) * TILE + n * hr, hr), hr)
        half_out[at, :] = part[away, :] + rs_in[0, at, :] + rs_in[1, at, :] + rs_in[2, at, :]
        over(n).start()
    for d in (1, 3, 2):
        to_x(d, 2).wait_recv()
    at = pl.ds(TILE, TILE)
    home = pl.ds(pl.multiple_of((2 * x + me.zh) * TILE, TILE), TILE)
    kept = part[home, :] + rs_in[0, at, :] + rs_in[1, at, :] + rs_in[2, at, :]
    load.wait()
    mine_rows = own[...]
    start = exact(mine_rows, w_self[...]) + bias[...]
    over(0).wait_recv()
    over(1).wait_recv()
    agg = kept + half_in[...]

    v = start + exact(agg, w_neigh[...])
    a = 0.7978845608028654
    b = 0.044715
    t = jnp.tanh(a * (v + b * (v * v * v)))
    hidden = 0.5 * v * (1.0 + t)
    scale = lax.rsqrt(jnp.mean(hidden * hidden, axis=-1, keepdims=True) + 1e-06)
    out[0] = hidden * scale
    g = cot[0]
    dot = jnp.mean(g * hidden, axis=-1, keepdims=True)
    d_hidden = scale * (g - hidden * (scale * scale * dot))
    slope = 0.5 * (1.0 + t) + 0.5 * v * (1.0 - t * t) * (a * (1.0 + 3.0 * b * (v * v)))
    d_pre = d_hidden * slope
    gb = jnp.sum(d_pre, axis=0, keepdims=True)

    first = jnp.broadcast_to(gb[:, :128], (PACK, 128))
    second = jnp.broadcast_to(gb[:, 128:], (PACK, 128))
    gbp = jnp.where(lax.broadcasted_iota(jnp.int32, (PACK, 128), 0) == 0, first, second)

    def pack(n, lhs):
        grad = exact(lhs, d_pre, ((0,), (0,)))
        packs[n, 0:128, :] = grad[:, :128]
        packs[n, 128:256, :] = grad[:, 128:]
        packs[n, 256:264, :] = gbp

    pack(1 - core, jnp.where(core == 0, agg, mine_rows))
    core_swap = remote(packs.at[1 - core], pack_in, c_send.at[0], c_recv.at[0], other)
    core_swap.start()
    pack(core, jnp.where(core == 0, mine_rows, agg))
    core_swap.wait_recv()
    b_now = gbp + pack_in[256:264, :]

    def piece(n, size):
        at = pl.ds(pl.multiple_of(n * size, size), size)
        return packs[core, at, :] + pack_in[at, :]

    for n in range(NX):
        xs[0, n, 0:64, :] = piece(n, 64)
        xs[0, n, 64:72, :] = b_now

    def x_copy(d):
        return remote(
            xs.at[0, lax.rem(x + d, NX)], xs.at[1, x], x_send.at[0, d], x_recv.at[0, x], x_dev[d]
        )

    def x_wait(d):
        src = lax.rem(x + NX - d, NX)
        remote(xs.at[0, 0], xs.at[1, src], x_send.at[0, d], x_recv.at[0, src], x_dev[d]).wait_recv()

    for d in (2, 1, 3):
        x_copy(d).start()
    xs[1, x] = xs[0, x]
    for d in (1, 3, 2):
        x_wait(d)
    x_sum = xs[1, 0] + xs[1, 1] + xs[1, 2] + xs[1, 3]

    for n in range(NY):
        ys[0, n, 0:8, :] = x_sum[n * 8 : n * 8 + 8]
        ys[0, n, 8:16, :] = x_sum[64:72]

    def y_copy(d):
        return remote(
            ys.at[0, lax.rem(y + d, NY)], ys.at[1, y], y_send.at[0, d], y_recv.at[0, y], y_dev[d]
        )

    def y_wait(d):
        src = lax.rem(y + NY - d, NY)
        remote(ys.at[0, 0], ys.at[1, src], y_send.at[0, d], y_recv.at[0, src], y_dev[d]).wait_recv()

    order = (4, 3, 5, 2, 6, 1, 7)
    for d in order:
        y_copy(d).start()
    ys[1, y] = ys[0, y]
    for d in order[::-1]:
        y_wait(d)
    y_sum = ys[1, 0]
    for n in range(1, NY):
        y_sum = y_sum + ys[1, n]

    zs[0] = y_sum
    zs[1 + z] = y_sum

    def z_copy(d):
        return remote(zs.at[0], zs.at[1 + z], z_send.at[d], z_recv.at[z], z_dev[d])

    def z_wait(d):
        src = lax.rem(z + NZ - d, NZ)
        remote(zs.at[0], zs.at[1 + src], z_send.at[d], z_recv.at[src], z_dev[d]).wait_recv()

    for d in order:
        z_copy(d).start()
    for d in order[::-1]:
        z_wait(d)
    z_sum = zs[1]
    for n in range(1, NZ):
        z_sum = z_sum + zs[1 + n]
    g_bias[:, 0:128] = z_sum[8:9]
    g_bias[:, 128:256] = z_sum[9:10]

    def at_y(n):
        return mine.at[core, pl.ds(pl.multiple_of(x * 64 + n * 8, 8), 8)]

    def y_back(d):
        return remote(at_y(y), at_y(y), y_send.at[1, d], y_recv.at[1, y], y_dev[d])

    def y_back_wait(d):
        src = lax.rem(y + NY - d, NY)
        remote(at_y(src), at_y(src), y_send.at[1, d], y_recv.at[1, src], y_dev[d]).wait_recv()

    mine[core, pl.ds(pl.multiple_of(x * 64 + y * 8, 8), 8), :] = z_sum[0:8]
    def at_x(n):
        return mine.at[core, pl.ds(pl.multiple_of(n * 64, 64), 64)]

    def x_back(d):
        return remote(at_x(x), at_x(x), x_send.at[1, d], x_recv.at[1, x], x_dev[d])

    def x_back_wait(d):
        src = lax.rem(x + NX - d, NX)
        remote(at_x(src), at_x(src), x_send.at[1, d], x_recv.at[1, src], x_dev[d]).wait_recv()

    def x_share(n):
        for d in (2, 1, 3):
            remote(at_y(n), at_y(n), x_send.at[1, d], x_recv.at[1, x], x_dev[d]).start()

    def core_share(n):
        remote(at_x(n), at_x(n), c_send.at[1], c_recv.at[1], other).start()

    for d in order:
        y_back(d).start()
    x_share(y)
    for d in order[::-1]:
        y_back_wait(d)
        x_share(lax.rem(y + NY - d, NY))
    core_share(x)
    for d in (1, 3, 2):
        x_back_wait(d)
        core_share(lax.rem(x + NX - d, NX))
    core_back = remote(mine.at[core], mine.at[core], c_send.at[1], c_recv.at[1], other)
    remote(mine.at[1 - core], mine.at[1 - core], c_send.at[1], c_recv.at[1], other).wait_recv()

    for d in (1, 2, 3):
        for n in range(3):
            to_x(d, n).wait_send()
        x_copy(d).wait_send()
        x_back(d).wait_send()
    over(0).wait_send()
    over(1).wait_send()
    core_swap.wait_send()
    core_back.wait_send()
    for d in range(1, 8):
        y_copy(d).wait_send()
        z_copy(d).wait_send()
        y_back(d).wait_send()


def finish(part, features, w_self, w_neigh, bias, cotangent):
    dma = pltpu.SemaphoreType.DMA
    vmem = pl.BlockSpec(memory_space=pltpu.VMEM)
    f32 = jnp.float32
    return pl.pallas_call(
        finish_kernel,
        out_shape=(
            jax.ShapeDtypeStruct((1, TILE, DOUT), f32),
            jax.ShapeDtypeStruct((2, 2 * DIN, 128), f32),
            jax.ShapeDtypeStruct((1, DOUT), f32),
        ),
        in_specs=[vmem, pl.BlockSpec(memory_space=pl.ANY), vmem, vmem, vmem, vmem],
        out_specs=(vmem, vmem, vmem),
        scratch_shapes=[
            pltpu.VMEM((TILE, DIN), f32),
            pltpu.VMEM((3, 2 * TILE, DIN), f32),
            pltpu.VMEM((TILE, DIN), f32),
            pltpu.VMEM((TILE, DIN), f32),
            pltpu.VMEM((2, 264, 128), f32),
            pltpu.VMEM((264, 128), f32),
            pltpu.VMEM((2, NX, 72, 128), f32),
            pltpu.VMEM((2, NY, 16, 128), f32),
            pltpu.VMEM((1 + NZ, 16, 128), f32),
            dma(()),
            dma((3, 3)),
            dma((3, 3)),
            dma((2,)),
            dma((2,)),
            dma((2,)),
            dma((2,)),
            dma((2, NX)),
            dma((2, NX)),
            dma((2, NY)),
            dma((2, NY)),
            dma((NZ,)),
            dma((NZ,)),
        ],
        compiler_params=pltpu.CompilerParams(
            collective_id=1, has_side_effects=True, vmem_limit_bytes=20 * 2**20
        ),
        name="finish",
    )(part, features, w_self, w_neigh, bias, cotangent)


def emit_kernel(o, m, b, out, g_self, g_neigh, g_bias, sems):
    moves = [(o, out), (b, g_bias)]
    for n, g in enumerate((g_self, g_neigh)):
        for h in range(2):
            moves.append((m.at[n, pl.ds(h * DIN, DIN)], g.at[:, pl.ds(h * 128, 128)]))
    copies = [pltpu.make_async_copy(src, dst, sems.at[i]) for i, (src, dst) in enumerate(moves)]
    for copy in copies:
        copy.start()
    for copy in copies:
        copy.wait()


def emit(out, grads, g_bias):
    f32 = jnp.float32
    vmem = pl.BlockSpec(memory_space=pltpu.VMEM)
    hbm = pl.BlockSpec(memory_space=pltpu.HBM)
    return pl.pallas_call(
        emit_kernel,
        out_shape=(
            jax.ShapeDtypeStruct((1, TILE, DOUT), f32),
            jax.ShapeDtypeStruct((DIN, DOUT), f32),
            jax.ShapeDtypeStruct((DIN, DOUT), f32),
            jax.ShapeDtypeStruct((1, DOUT), f32),
        ),
        in_specs=[vmem, vmem, vmem],
        out_specs=(hbm, hbm, hbm, hbm),
        scratch_shapes=[pltpu.SemaphoreType.DMA((6,))],
        compiler_params=pltpu.CompilerParams(vmem_limit_bytes=4 * 2**20),
        name="emit",
    )(out, grads, g_bias)


def on_device(
    features, self_weight, neigh_weight, bias, edge_tiles, tile_rows, tile_cols, tile_count, cotangent
):
    got = spread(pltpu.with_memory_space_constraint(features, pltpu.HBM))
    part = products(tile_rows, tile_cols, tile_count, got, edge_tiles)
    done = finish(part, features, self_weight, neigh_weight, bias.reshape(1, DOUT), cotangent)
    out, gs, gn, gb = emit(*done)
    return out, gs, gn, gb.reshape(DOUT)


def solution(mesh):
    in_specs = (
        P("col", None, None),
        P(),
        P(),
        P(),
        P("row", "col", None, None, None),
        P("row", "col", None),
        P("row", "col", None),
        P("row", "col", None),
        P("col", "row", None),
    )
    out_specs = (P("col", "row", None), P(), P(), P())
    return jax.shard_map(on_device, mesh=mesh, in_specs=in_specs, out_specs=out_specs, check_vma=False)
```

```python
import jax
import jax.numpy as jnp
from jax import lax
from jax.experimental import pallas as pl
from jax.experimental.pallas import tpu as pltpu
from jax.sharding import PartitionSpec as P

MESH = pl.DeviceIdType.MESH
TILE = 128
KT = 8
G = 1024
DIN = 128
DOUT = 256
STOPS = 8
TS = 12
NX, NY, NZ = 4, 8, 8
PR = G // NX
NS = 4
PART = PR // NS
PACK = 8


class Place:
    def __init__(self):
        self.r = lax.axis_index("row")
        c = lax.axis_index("col")
        self.x = lax.div(self.r, 2)
        self.zh = lax.rem(self.r, 2)
        self.y = lax.div(c, 8)
        k = lax.rem(c, 8)
        self.zl = lax.div(k, 2)
        self.core = lax.rem(k, 2)
        self.z = self.zh * 4 + self.zl

    def dev(self, x=None, y=None, z=None, core=None):
        x = self.x if x is None else x
        y = self.y if y is None else y
        z = self.z if z is None else z
        core = self.core if core is None else core
        return (x * 2 + lax.div(z, 4), y * 8 + lax.rem(z, 4) * 2 + core)


def rows_of(ref, plane, p, rows=PR):
    return ref.at[plane, pl.ds(pl.multiple_of(p * rows, rows), rows)]


def remote(src, dst, send, recv, dev):
    return pltpu.make_async_remote_copy(
        src_ref=src, dst_ref=dst, send_sem=send, recv_sem=recv, device_id=dev, device_id_type=MESH
    )


def greet(devs):
    barrier = pltpu.get_barrier_semaphore()
    for dev in devs:
        pl.semaphore_signal(barrier, inc=1, device_id=dev, device_id_type=MESH)
    return barrier


def spread_kernel(
    feat,
    got,
    walk,
    walk2,
    b_buf,
    y_send,
    y_recv,
    w_send,
    w_recv,
    x_send,
    ab_recv,
    x2_send,
    seam_send,
    z_send,
    g_recv,
    s_send,
    s_recv,
    loc,
):
    me = Place()
    x, z, zl, zh, core = me.x, me.z, me.zl, me.zh, me.core
    y_at = {d: me.dev(y=lax.rem(me.y + d, NY)) for d in (1, 2, 6, 7)}
    z_at = {d: me.dev(z=lax.rem(z + d, NZ)) for d in (1, 2, 6, 7)}
    x_at = [me.dev(x=lax.rem(x + d, NX)) for d in range(NX)]
    other = me.dev(core=1 - core)
    low_seam = z == 3
    high_seam = z == 4
    seam = jnp.logical_or(low_seam, high_seam)
    far = jnp.where(low_seam, 4, 3)
    barrier = greet(list(y_at.values()) + list(z_at.values()) + x_at[1:] + [other])

    @pl.when(seam)
    def _():
        greet([me.dev(x=lax.rem(x + d, NX), z=far) for d in range(1, NX)])

    load = pltpu.make_async_copy(feat.at[0, pl.ds(pl.multiple_of(x * PR, PR), PR)], walk.at[0], loc)
    load.start()
    load.wait()
    pl.semaphore_wait(barrier, 12 + 3 * seam.astype(jnp.int32))

    def y_copy(src, dst, d):
        return remote(walk.at[src], walk.at[dst], y_send.at[dst], y_recv.at[dst, 0], y_at[d])

    def y_part(src, dst, d, s):
        at = pl.ds(s * PART, PART)
        return remote(walk.at[src, at], walk.at[dst, at], y_send.at[dst], y_recv.at[dst, s], y_at[d])

    half = PR // 2

    def piece(plane, p, j=None):
        ref = b_buf if plane == 1 else got.at[plane]
        if j is None:
            return ref.at[pl.ds(pl.multiple_of(p * PR, PR), PR)]
        return ref.at[pl.ds(pl.multiple_of(p * PR + j * half, half), half)]

    def walked(h, j):
        return walk.at[h] if j is None else walk.at[h, pl.ds(j * half, half)]

    def x_copy(h, v, j):
        to = h // 2 if v == 0 else lax.rem(h // 2 - zh + NX, NX)
        dev = me.dev(x=jnp.int32(to))
        return to, remote(walked(h, j), piece(v, x, j), x_send.at[h], ab_recv.at[v, x, j or 0], dev)

    def seam_copy(h, low, j):
        to = lax.rem(jnp.int32(h // 2 + (NX - 1 if low else 0)), NX)
        plane = 2 if low else 6
        side = 0 if low else 1
        dev = me.dev(x=to, z=jnp.int32(4 if low else 3))
        return remote(walked(h, j), piece(plane, x, j), seam_send.at[h], g_recv.at[side, x], dev)

    def across(h, j=None, finish=False):
        for v in (0, 1):
            fits = zh == h % 2 if v == 0 else zh != h % 2

            @pl.when(fits)
            def _():
                to, copy = x_copy(h, v, j)

                @pl.when(to != x)
                def _():
                    copy.wait_send() if finish else copy.start()

                if not finish:

                    @pl.when(to == x)
                    def _():
                        pltpu.make_async_copy(walked(h, j), piece(v, x, j), ab_recv.at[v, x, j]).start()

        if h % 2 == 0:
            for low, fits in ((True, low_seam), (False, high_seam)):

                @pl.when(fits)
                def _():
                    copy = seam_copy(h, low, j)
                    copy.wait_send() if finish else copy.start()

    def up_copy(p, j=None):
        return remote(piece(0, p, j), piece(2, p, j), z_send.at[0, p], g_recv.at[0, p], z_at[1])

    def down_copy(p, j=None):
        return remote(piece(1, p, j), piece(6, p, j), z_send.at[1, p], g_recv.at[1, p], z_at[7])

    def own_swap(v, p):
        return remote(piece(v, p), rows_of(got, 1, p), s_send.at[0], s_recv.at[0], other)

    def swap(n, p):
        return remote(rows_of(got, 2 * n, p), rows_of(got, 2 * n + 1, p), s_send.at[n], s_recv.at[n], other)

    def swapped(n):
        return remote(got.at[2 * n], got.at[2 * n + 1], s_send.at[n], s_recv.at[n], other)

    def pass_on(v):
        for j in range(2):
            for p in range(NX):
                remote(walked(0, j), piece(v, p, j), x_send.at[0], ab_recv.at[v, p, j], other).wait_recv()

                @pl.when(jnp.logical_not(low_seam if v == 0 else high_seam))
                def _():
                    (up_copy(p, j) if v == 0 else down_copy(p, j)).start()

                if j == 1:

                    @pl.when(core == v)
                    def _():
                        own_swap(v, p).start()

    near_a = jnp.minimum(me.r, 8 - me.r)
    next_r = lax.rem(me.r + 1, 8)
    near_b = jnp.minimum(next_r, 8 - next_r)

    def pass_near(n):
        for v, near in ((0, near_a), (1, near_b)):

            @pl.when(near == n)
            def _():
                pass_on(v)

    even = jnp.logical_xor(zl >= 2, zh == 1)
    two = jnp.where(core == 0, 2, 6)
    ahead = remote(walk.at[0], walk2.at[0], w_send.at[0], w_recv.at[0], me.dev(z=lax.rem(z + two, NZ)))
    def w_copy(src, dst, d):
        return remote(walk2.at[src], walk2.at[dst], w_send.at[dst], w_recv.at[dst], y_at[d])

    def w_half(src, dst, d, n):
        at = pl.ds(n * half, half)
        sem = dst if n == 0 else 8
        return remote(walk2.at[src, at], walk2.at[dst, at], w_send.at[sem], w_recv.at[sem], y_at[d])

    def across2(h, finish=False):
        to = jnp.where(zl >= 2, h // 2, lax.rem(h // 2 - zh + NX, NX))
        copy = remote(walk2.at[h], rows_of(got, 4, x), x2_send.at[h], g_recv.at[2, x], me.dev(x=to))

        @pl.when(to != x)
        def _():
            copy.wait_send() if finish else copy.start()

        if not finish:

            @pl.when(to == x)
            def _():
                pltpu.make_async_copy(walk2.at[h], rows_of(got, 4, x), g_recv.at[2, x]).start()

    def w_start():
        ahead.wait_recv()

        @pl.when(even)
        def _():
            w_copy(0, 2, 2).start()
            w_copy(0, 6, 6).start()
            across2(0)

        @pl.when(jnp.logical_not(even))
        def _():
            w_copy(0, 1, 1).start()
            w_copy(0, 7, 7).start()

    def w_near():
        @pl.when(even)
        def _():
            w_copy(2, 2, 2).wait_recv()
            w_half(2, 4, 2, 0).start()
            w_copy(6, 6, 6).wait_recv()
            w_half(6, 4, 6, 1).start()
            across2(2)
            across2(6)

        @pl.when(jnp.logical_not(even))
        def _():
            w_copy(1, 1, 1).wait_recv()
            w_copy(1, 3, 2).start()
            w_copy(7, 7, 7).wait_recv()
            w_copy(7, 5, 6).start()
            across2(1)
            across2(7)

    def w_far():
        @pl.when(even)
        def _():
            w_half(2, 4, 2, 0).wait_recv()
            w_half(6, 4, 6, 1).wait_recv()
            across2(4)

        @pl.when(jnp.logical_not(even))
        def _():
            w_copy(3, 3, 2).wait_recv()
            across2(3)
            w_copy(5, 5, 6).wait_recv()
            across2(5)

    for s in range(NS):
        y_part(0, 1, 1, s).start()
        y_part(0, 7, 7, s).start()
    ahead.start()
    across(0, 0)
    across(0, 1)
    for n in range(1, 5):
        for s in range(NS):
            first = s < NS // 2
            if n < 4 or first:
                y_part(n, n, 1, s).wait_recv()
            if n < 3 or (n == 3 and first):
                y_part(n, n + 1, 1, s).start()
            if n < 4 or not first:
                y_part(8 - n, 8 - n, 7, s).wait_recv()
            if n < 3 or (n == 3 and not first):
                y_part(8 - n, 7 - n, 7, s).start()
            if s % (NS // 2) == NS // 2 - 1:
                across(n, s // (NS // 2))
                if n < 4:
                    across(8 - n, s // (NS // 2))
        if n == 3:
            w_start()
        if n >= 2:
            pass_near(n - 2)
    w_near()
    pass_near(3)
    pass_near(4)
    w_far()

    for p in range(NX):
        up_copy(p).wait_recv()
        swap(1, p).start()
        down_copy(p).wait_recv()
        swap(3, p).start()
    for p in range(NX):
        remote(walk.at[0], rows_of(got, 4, p), x2_send.at[0], g_recv.at[2, p], other).wait_recv()
        swap(2, p).start()

    for n in (0, 1, 3, 2):
        swapped(n).wait_recv()
        swapped(n).wait_send()
    for p in range(NX):

        @pl.when(jnp.logical_not(low_seam))
        def _():
            up_copy(p).wait_send()

        @pl.when(jnp.logical_not(high_seam))
        def _():
            down_copy(p).wait_send()

    for h in range(8):
        across(h, finish=True)
        if h:
            y_copy(h, h, 1).wait_send()
    ahead.wait_send()

    @pl.when(even)
    def _():
        for h in (0, 2, 4, 6):
            across2(h, finish=True)
        w_copy(2, 2, 2).wait_send()
        w_copy(6, 6, 6).wait_send()
        w_half(2, 4, 2, 0).wait_send()
        w_half(6, 4, 6, 1).wait_send()

    @pl.when(jnp.logical_not(even))
    def _():
        for h in (1, 3, 5, 7):
            across2(h, finish=True)
            w_copy(h, h, 1).wait_send()


def spread(features):
    dma = pltpu.SemaphoreType.DMA
    return pl.pallas_call(
        spread_kernel,
        out_shape=jax.ShapeDtypeStruct((8, G, DIN), jnp.float32),
        in_specs=[pl.BlockSpec(memory_space=pltpu.HBM)],
        out_specs=pl.BlockSpec(memory_space=pltpu.VMEM),
        scratch_shapes=[
            pltpu.VMEM((8, PR, DIN), jnp.float32),
            pltpu.VMEM((8, PR, DIN), jnp.float32),
            pltpu.VMEM((G, DIN), jnp.float32),
            dma((8,)),
            dma((8, NS)),
            dma((9,)),
            dma((9,)),
            dma((8,)),
            dma((2, NX, 2)),
            dma((8,)),
            dma((8,)),
            dma((2, NX)),
            dma((3, NX)),
            dma((4,)),
            dma((4,)),
            dma(()),
        ],
        compiler_params=pltpu.CompilerParams(
            collective_id=0, has_side_effects=True, vmem_limit_bytes=20 * 2**20
        ),
        name="spread",
    )(features)


def products_kernel(rows, cols, counts, got, tiles, part):
    core = lax.rem(lax.axis_index("col"), 2)
    part[...] = jnp.zeros_like(part)

    def stop(s, carry):
        plane = jnp.where(jnp.logical_and(core == 0, lax.rem(s, 2) == 1), lax.rem(s + 2, 8), s)
        count = counts[0, 0, s]
        prods = []
        for t in range(TS):
            q = s * TS + t
            col = pl.multiple_of(cols[0, 0, q] * TILE, TILE)
            chosen = got[plane, pl.ds(col, TILE), :]
            chosen = jnp.where(t < count, chosen, 0.0)
            high = chosen.astype(jnp.bfloat16)
            low = (chosen - high.astype(jnp.float32)).astype(jnp.bfloat16)
            both = jnp.dot(
                tiles[0, 0, q], jnp.concatenate([high, low], axis=1), preferred_element_type=jnp.float32
            )
            prods.append(both[:, :DIN] + both[:, DIN:])
        for t in range(TS):
            at = pl.ds(pl.multiple_of(rows[0, 0, s * TS + t] * TILE, TILE), TILE)
            part[at, :] = part[at, :] + prods[t]
        return carry

    lax.fori_loop(0, STOPS, stop, 0)


def products(rows, cols, counts, got, tiles):
    smem = pl.BlockSpec(memory_space=pltpu.SMEM)
    vmem = pl.BlockSpec(memory_space=pltpu.VMEM)
    return pl.pallas_call(
        products_kernel,
        out_shape=jax.ShapeDtypeStruct((G, DIN), jnp.float32),
        in_specs=[smem, smem, smem, vmem, vmem],
        out_specs=vmem,
        compiler_params=pltpu.CompilerParams(vmem_limit_bytes=20 * 2**20),
        name="products",
    )(rows, cols, counts, got, tiles)


def split(a):
    high = a.astype(jnp.bfloat16)
    return high, (a - high.astype(jnp.float32)).astype(jnp.bfloat16)


def exact(a, b, dims=((1,), (0,))):
    def dot(p, q):
        return lax.dot_general(p, q, (dims, ((), ())), preferred_element_type=jnp.float32)

    a_high, a_low = split(a)
    b_high, b_low = split(b)
    return dot(a_high, b_high) + (dot(a_high, b_low) + dot(a_low, b_high))


def finish_kernel(
    part,
    feat,
    w_self,
    w_neigh,
    bias,
    cot,
    out,
    mine,
    g_bias,
    own,
    rs_in,
    half_in,
    half_out,
    packs,
    pack_in,
    xs,
    ys,
    zs,
    loc,
    rs_send,
    rs_recv,
    h_send,
    h_recv,
    c_send,
    c_recv,
    x_send,
    x_recv,
    y_send,
    y_recv,
    z_send,
    z_recv,
):
    me = Place()
    r, x, y, z, core = me.r, me.x, me.y, me.z, me.core
    x_dev = [me.dev(x=lax.rem(x + d, NX)) for d in range(NX)]
    y_dev = [me.dev(y=lax.rem(y + d, NY)) for d in range(NY)]
    z_dev = [me.dev(z=lax.rem(z + d, NZ)) for d in range(NZ)]
    other = me.dev(core=1 - core)
    barrier = greet(x_dev[1:] + y_dev[1:] + z_dev[1:] + [other])
    load = pltpu.make_async_copy(feat.at[0, pl.ds(pl.multiple_of(r * TILE, TILE), TILE)], own, loc)
    load.start()
    pl.semaphore_wait(barrier, NX + NY + NZ - 2)

    hr = TILE // 2

    def to_x(d, n):
        there = 2 * lax.rem(x + d, NX)
        if n < 2:
            src = part.at[pl.ds(pl.multiple_of((there + 1 - me.zh) * TILE + n * hr, hr), hr)]
            dst = rs_in.at[d - 1, pl.ds(n * hr, hr)]
        else:
            src = part.at[pl.ds(pl.multiple_of((there + me.zh) * TILE, TILE), TILE)]
            dst = rs_in.at[d - 1, pl.ds(TILE, TILE)]
        return remote(src, dst, rs_send.at[d - 1, n], rs_recv.at[d - 1, n], x_dev[d])

    def over(n):
        at = pl.ds(n * hr, hr)
        return remote(half_out.at[at], half_in.at[at], h_send.at[n], h_recv.at[n], z_dev[4])

    for n in range(3):
        for d in (2, 1, 3):
            to_x(d, n).start()
    for n in range(2):
        for d in (1, 3, 2):
            to_x(d, n).wait_recv()
        at = pl.ds(n * hr, hr)
        away = pl.ds(pl.multiple_of((2 * x + 1 - me.zh) * TILE + n * hr, hr), hr)
        half_out[at, :] = part[away, :] + rs_in[0, at, :] + rs_in[1, at, :] + rs_in[2, at, :]
        over(n).start()
    for d in (1, 3, 2):
        to_x(d, 2).wait_recv()
    at = pl.ds(TILE, TILE)
    home = pl.ds(pl.multiple_of((2 * x + me.zh) * TILE, TILE), TILE)
    kept = part[home, :] + rs_in[0, at, :] + rs_in[1, at, :] + rs_in[2, at, :]
    load.wait()
    mine_rows = own[...]
    start = exact(mine_rows, w_self[...]) + bias[...]
    over(0).wait_recv()
    over(1).wait_recv()
    agg = kept + half_in[...]

    v = start + exact(agg, w_neigh[...])
    a = 0.7978845608028654
    b = 0.044715
    t = jnp.tanh(a * (v + b * (v * v * v)))
    hidden = 0.5 * v * (1.0 + t)
    scale = lax.rsqrt(jnp.mean(hidden * hidden, axis=-1, keepdims=True) + 1e-06)
    out[0] = hidden * scale
    g = cot[0]
    dot = jnp.mean(g * hidden, axis=-1, keepdims=True)
    d_hidden = scale * (g - hidden * (scale * scale * dot))
    slope = 0.5 * (1.0 + t) + 0.5 * v * (1.0 - t * t) * (a * (1.0 + 3.0 * b * (v * v)))
    d_pre = d_hidden * slope
    gb = jnp.sum(d_pre, axis=0, keepdims=True)

    first = jnp.broadcast_to(gb[:, :128], (PACK, 128))
    second = jnp.broadcast_to(gb[:, 128:], (PACK, 128))
    gbp = jnp.where(lax.broadcasted_iota(jnp.int32, (PACK, 128), 0) == 0, first, second)

    def pack(n, lhs):
        grad = exact(lhs, d_pre, ((0,), (0,)))
        packs[n, 0:128, :] = grad[:, :128]
        packs[n, 128:256, :] = grad[:, 128:]
        packs[n, 256:264, :] = gbp

    pack(1 - core, jnp.where(core == 0, agg, mine_rows))
    core_swap = remote(packs.at[1 - core], pack_in, c_send.at[0], c_recv.at[0], other)
    core_swap.start()
    pack(core, jnp.where(core == 0, mine_rows, agg))
    core_swap.wait_recv()
    b_now = gbp + pack_in[256:264, :]

    def piece(n, size):
        at = pl.ds(pl.multiple_of(n * size, size), size)
        return packs[core, at, :] + pack_in[at, :]

    for n in range(NX):
        xs[0, n, 0:64, :] = piece(n, 64)
        xs[0, n, 64:72, :] = b_now

    def x_copy(d):
        return remote(
            xs.at[0, lax.rem(x + d, NX)], xs.at[1, x], x_send.at[0, d], x_recv.at[0, x], x_dev[d]
        )

    def x_wait(d):
        src = lax.rem(x + NX - d, NX)
        remote(xs.at[0, 0], xs.at[1, src], x_send.at[0, d], x_recv.at[0, src], x_dev[d]).wait_recv()

    for d in (2, 1, 3):
        x_copy(d).start()
    xs[1, x] = xs[0, x]
    for d in (1, 3, 2):
        x_wait(d)
    x_sum = xs[1, 0] + xs[1, 1] + xs[1, 2] + xs[1, 3]

    for n in range(NY):
        ys[0, n, 0:8, :] = x_sum[n * 8 : n * 8 + 8]
        ys[0, n, 8:16, :] = x_sum[64:72]

    def y_copy(d):
        return remote(
            ys.at[0, lax.rem(y + d, NY)], ys.at[1, y], y_send.at[0, d], y_recv.at[0, y], y_dev[d]
        )

    def y_wait(d):
        src = lax.rem(y + NY - d, NY)
        remote(ys.at[0, 0], ys.at[1, src], y_send.at[0, d], y_recv.at[0, src], y_dev[d]).wait_recv()

    order = (4, 3, 5, 2, 6, 1, 7)
    for d in order:
        y_copy(d).start()
    ys[1, y] = ys[0, y]
    for d in order[::-1]:
        y_wait(d)
    y_sum = ys[1, 0]
    for n in range(1, NY):
        y_sum = y_sum + ys[1, n]

    zs[0] = y_sum
    zs[1 + z] = y_sum

    def z_copy(d):
        return remote(zs.at[0], zs.at[1 + z], z_send.at[d], z_recv.at[z], z_dev[d])

    def z_wait(d):
        src = lax.rem(z + NZ - d, NZ)
        remote(zs.at[0], zs.at[1 + src], z_send.at[d], z_recv.at[src], z_dev[d]).wait_recv()

    for d in order:
        z_copy(d).start()
    for d in order[::-1]:
        z_wait(d)
    z_sum = zs[1]
    for n in range(1, NZ):
        z_sum = z_sum + zs[1 + n]
    g_bias[:, 0:128] = z_sum[8:9]
    g_bias[:, 128:256] = z_sum[9:10]

    def at_y(n):
        return mine.at[core, pl.ds(pl.multiple_of(x * 64 + n * 8, 8), 8)]

    def y_back(d):
        return remote(at_y(y), at_y(y), y_send.at[1, d], y_recv.at[1, y], y_dev[d])

    def y_back_wait(d):
        src = lax.rem(y + NY - d, NY)
        remote(at_y(src), at_y(src), y_send.at[1, d], y_recv.at[1, src], y_dev[d]).wait_recv()

    mine[core, pl.ds(pl.multiple_of(x * 64 + y * 8, 8), 8), :] = z_sum[0:8]
    def at_x(n):
        return mine.at[core, pl.ds(pl.multiple_of(n * 64, 64), 64)]

    def x_back(d):
        return remote(at_x(x), at_x(x), x_send.at[1, d], x_recv.at[1, x], x_dev[d])

    def x_back_wait(d):
        src = lax.rem(x + NX - d, NX)
        remote(at_x(src), at_x(src), x_send.at[1, d], x_recv.at[1, src], x_dev[d]).wait_recv()

    def x_share(n):
        for d in (2, 1, 3):
            remote(at_y(n), at_y(n), x_send.at[1, d], x_recv.at[1, x], x_dev[d]).start()

    def core_share(n):
        remote(at_x(n), at_x(n), c_send.at[1], c_recv.at[1], other).start()

    for d in order:
        y_back(d).start()
    x_share(y)
    for d in order[::-1]:
        y_back_wait(d)
        x_share(lax.rem(y + NY - d, NY))
    core_share(x)
    for d in (1, 3, 2):
        x_back_wait(d)
        core_share(lax.rem(x + NX - d, NX))
    core_back = remote(mine.at[core], mine.at[core], c_send.at[1], c_recv.at[1], other)
    remote(mine.at[1 - core], mine.at[1 - core], c_send.at[1], c_recv.at[1], other).wait_recv()

    for d in (1, 2, 3):
        for n in range(3):
            to_x(d, n).wait_send()
        x_copy(d).wait_send()
        x_back(d).wait_send()
    over(0).wait_send()
    over(1).wait_send()
    core_swap.wait_send()
    core_back.wait_send()
    for d in range(1, 8):
        y_copy(d).wait_send()
        z_copy(d).wait_send()
        y_back(d).wait_send()


def finish(part, features, w_self, w_neigh, bias, cotangent):
    dma = pltpu.SemaphoreType.DMA
    vmem = pl.BlockSpec(memory_space=pltpu.VMEM)
    f32 = jnp.float32
    return pl.pallas_call(
        finish_kernel,
        out_shape=(
            jax.ShapeDtypeStruct((1, TILE, DOUT), f32),
            jax.ShapeDtypeStruct((2, 2 * DIN, 128), f32),
            jax.ShapeDtypeStruct((1, DOUT), f32),
        ),
        in_specs=[vmem, pl.BlockSpec(memory_space=pl.ANY), vmem, vmem, vmem, vmem],
        out_specs=(vmem, vmem, vmem),
        scratch_shapes=[
            pltpu.VMEM((TILE, DIN), f32),
            pltpu.VMEM((3, 2 * TILE, DIN), f32),
            pltpu.VMEM((TILE, DIN), f32),
            pltpu.VMEM((TILE, DIN), f32),
            pltpu.VMEM((2, 264, 128), f32),
            pltpu.VMEM((264, 128), f32),
            pltpu.VMEM((2, NX, 72, 128), f32),
            pltpu.VMEM((2, NY, 16, 128), f32),
            pltpu.VMEM((1 + NZ, 16, 128), f32),
            dma(()),
            dma((3, 3)),
            dma((3, 3)),
            dma((2,)),
            dma((2,)),
            dma((2,)),
            dma((2,)),
            dma((2, NX)),
            dma((2, NX)),
            dma((2, NY)),
            dma((2, NY)),
            dma((NZ,)),
            dma((NZ,)),
        ],
        compiler_params=pltpu.CompilerParams(
            collective_id=1, has_side_effects=True, vmem_limit_bytes=20 * 2**20
        ),
        name="finish",
    )(part, features, w_self, w_neigh, bias, cotangent)


def emit_kernel(o, m, b, out, g_self, g_neigh, g_bias, sems):
    moves = [(o, out), (b, g_bias)]
    for n, g in enumerate((g_self, g_neigh)):
        for h in range(2):
            moves.append((m.at[n, pl.ds(h * DIN, DIN)], g.at[:, pl.ds(h * 128, 128)]))
    copies = [pltpu.make_async_copy(src, dst, sems.at[i]) for i, (src, dst) in enumerate(moves)]
    for copy in copies:
        copy.start()
    for copy in copies:
        copy.wait()


def emit(out, grads, g_bias):
    f32 = jnp.float32
    vmem = pl.BlockSpec(memory_space=pltpu.VMEM)
    hbm = pl.BlockSpec(memory_space=pltpu.HBM)
    return pl.pallas_call(
        emit_kernel,
        out_shape=(
            jax.ShapeDtypeStruct((1, TILE, DOUT), f32),
            jax.ShapeDtypeStruct((DIN, DOUT), f32),
            jax.ShapeDtypeStruct((DIN, DOUT), f32),
            jax.ShapeDtypeStruct((1, DOUT), f32),
        ),
        in_specs=[vmem, vmem, vmem],
        out_specs=(hbm, hbm, hbm, hbm),
        scratch_shapes=[pltpu.SemaphoreType.DMA((6,))],
        compiler_params=pltpu.CompilerParams(vmem_limit_bytes=4 * 2**20),
        name="emit",
    )(out, grads, g_bias)


def on_device(
    features, self_weight, neigh_weight, bias, edge_tiles, tile_rows, tile_cols, tile_count, cotangent
):
    got = spread(pltpu.with_memory_space_constraint(features, pltpu.HBM))
    part = products(tile_rows, tile_cols, tile_count, got, edge_tiles)
    done = finish(part, features, self_weight, neigh_weight, bias.reshape(1, DOUT), cotangent)
    out, gs, gn, gb = emit(*done)
    return out, gs, gn, gb.reshape(DOUT)


def solution(mesh):
    in_specs = (
        P("col", None, None),
        P(),
        P(),
        P(),
        P("row", "col", None, None, None),
        P("row", "col", None),
        P("row", "col", None),
        P("row", "col", None),
        P("col", "row", None),
    )
    out_specs = (P("col", "row", None), P(), P(), P())
    return jax.shard_map(on_device, mesh=mesh, in_specs=in_specs, out_specs=out_specs, check_vma=False)
```
